128 devices in a mesh: chan: 4 (over x_hi, core), half: 2 (over x_lo), ctx: 16 (over z, y).
Axes of the slice: x: 4 (x_hi: 2, x_lo: 2; x = x_hi * 2 + x_lo), y: 4, z: 4, core: 2. Of those that a mesh axis runs over, the one named last changes fastest.
Arguments:
- query_gate: bfloat16 [8192, 8192], P('ctx', 'chan'), parts along dimension 1, may hold values from -6 to 6
- key_gate: bfloat16 [8192, 8192], P('ctx', 'chan'), parts along dimension 1, may hold values from -6 to 6
- value_input: bfloat16 [8192, 8192], P('ctx', 'chan'), parts along dimension 1, may hold values from -6 to 6
- residues: float32 [16, 8192], P(None, 'chan'), parts along dimension 1, may hold values from -1.5 to 1.5
- decays: float32 [16, 8192], P(None, 'chan'), parts along dimension 1, may hold values from 6.1035157e-06 to 0.05
- skip_gain: float32 [8192], P('chan'), parts along dimension 0, may hold values from 0.25 to 1
Outputs:
- mixed: bfloat16 [8192, 8192], P('ctx', 'chan'), parts along dimension 1
The draws below stay inside these ranges and needn't reach their ends.
There are 4 independent parts, one for each index of `chan`. The reference program is written for one: setup_inputs(seed, part) draws one part's arguments, and reference() takes and returns one part's arrays. A program takes and returns all parts, laid end to end along the dimension named above; each array names one. Nothing has to cross between parts.
All inputs are finite; a program needn't handle non-finite values.
Results may differ from the reference program's by a relative error of at most 0.00155.
Values may be sent and summed in bfloat16 or wider, within the bound.
A program may use at most 128 MiB of HBM per device.

```python
import math
import jax
import jax.numpy as jnp

CHANNELS = 2048
MODES = 16
SEQ = 8192


def levels(stream_key, extent, shards, low, top_value):
    def one(position, blocks):
        steps = jax.random.uniform(jax.random.fold_in(jax.random.fold_in(stream_key, 6), position), (blocks,), jnp.float32, low / len(shards), top_value / len(shards))
        return jnp.repeat(jnp.exp(steps), extent[position] // blocks).reshape((-1,) + (1,) * (len(extent) - position - 1))

    level = one(*shards[0])
    for cut in shards[1:]:
        level = level * one(*cut)
    return level


def noise(stream_key, shape, deviation, most, cuts=(), kind=jnp.bfloat16):
    result = deviation * jax.random.normal(stream_key, shape, jnp.float32)
    if cuts:
        result = result * levels(stream_key, shape, cuts, -0.22, 0.18)
    return jnp.clip(result, -most, most).astype(kind)


def setup_inputs(seed: int = 0, part: int = 0) -> dict:
    keys = jax.random.split(jax.random.key(seed), 7)
    own_keys = jax.random.split(jax.random.fold_in(keys[6], part), 7)
    query_gate = noise(own_keys[0], (SEQ, CHANNELS), 1.0, 6.0, ((0, 16),))
    key_gate = noise(own_keys[1], (SEQ, CHANNELS), 1.0, 6.0, ((0, 16),))
    value_input = noise(own_keys[2], (SEQ, CHANNELS), 1.0, 6.0, ((0, 16),))
    residues = noise(own_keys[3], (MODES, CHANNELS), MODES ** -0.5, 1.5, (), jnp.float32)
    decays = jnp.clip(jnp.exp(jax.random.uniform(own_keys[4], (MODES, CHANNELS), jnp.float32, math.log(6.10351571594947e-06), math.log(0.05))), 6.10351571594947e-06, 0.05)
    skip_gain = jnp.clip(jax.random.uniform(own_keys[5], (CHANNELS,), jnp.float32, 0.25, 1.0), 0.25, 1.0)
    return {"query_gate": query_gate, "key_gate": key_gate, "value_input": value_input, "residues": residues, "decays": decays, "skip_gain": skip_gain}


def reference(query_gate, key_gate, value_input, residues, decays, skip_gain):
    signal = key_gate.astype(jnp.float32) * value_input.astype(jnp.float32)
    steps_time = jnp.arange(SEQ, dtype=jnp.float32)[:, None]
    kernel = jnp.zeros((SEQ, CHANNELS), jnp.float32)
    for mode_idx in range(MODES):
        kernel = kernel + residues[mode_idx] * jnp.sqrt(decays[mode_idx]) * jnp.exp(-decays[mode_idx] * steps_time)
    spec_signal = jnp.fft.rfft(signal, n=2 * SEQ, axis=0)
    spec_kernel = jnp.fft.rfft(kernel, n=2 * SEQ, axis=0)
    conv_out = jnp.fft.irfft(spec_signal * spec_kernel, n=2 * SEQ, axis=0)[:SEQ].astype(jnp.float32)
    return (query_gate.astype(jnp.float32) * (conv_out + skip_gain * signal)).astype(jnp.bfloat16)
```

```python
import jax
import jax.numpy as jnp
from jax import lax
from jax.experimental import pallas as pl
from jax.experimental.pallas import tpu as pltpu
from jax.sharding import PartitionSpec as P

F32 = jnp.float32
LANES = 128
SUBS = 8
STEP = 16
CHUNKS = 4


def make_kernel(rows, group, modes, ctx_size):
    chunk = rows // CHUNKS
    span = rows + STEP

    def kernel(
        q_hbm, k_hbm, v_hbm, r_hbm, d_hbm, g_ref, o_hbm,
        kb, vb, qb, ob, rb, db, xb, rate, fade, amp, ends, heard, starts, enter,
        p_sem, k_sem, v_sem, q_sem, o_sem, e_send, e_recv, s_send, s_recv, t_send, t_recv,
    ):
        half = lax.axis_index("half")
        ctx = lax.axis_index("ctx")
        owner = (half, 1 - half)

        def columns(place):
            return pl.ds(pl.multiple_of(owner[place] * group, group), group)

        def load(hbm, buf, sem, place, c):
            at = pl.ds(c * chunk, chunk)
            return pltpu.make_async_copy(hbm.at[at, columns(place)], buf.at[place, at, :], sem.at[place, c])

        def store(place, c):
            at = pl.ds(c * chunk, chunk)
            return pltpu.make_async_copy(ob.at[place, at, :], o_hbm.at[at, columns(place)], o_sem.at[place, c])

        def remote(src, dst, send_sem, recv_sem, to_half, to_ctx):
            return pltpu.make_async_remote_copy(
                src_ref=src,
                dst_ref=dst,
                send_sem=send_sem,
                recv_sem=recv_sem,
                device_id={"half": to_half, "ctx": to_ctx},
                device_id_type=pl.DeviceIdType.MESH,
            )

        def peer(d):
            return lax.rem(ctx + d, ctx_size)

        def to_owner(d):
            return remote(ends.at[peer(d)], heard.at[ctx], e_send.at[d], e_recv.at[d], half, peer(d))

        def to_same(d):
            return remote(starts.at[peer(d)], enter.at[0, ctx], s_send.at[d], s_recv.at[d], half, peer(d))

        def to_twin(d):
            return remote(starts.at[peer(d)], enter.at[1, ctx], t_send.at[d], t_recv.at[d], 1 - half, peer(d))

        def each(first, act):
            def body(d, carry):
                act(d)
                return carry

            lax.fori_loop(first, ctx_size, body, 0)

        barrier = pltpu.get_barrier_semaphore()

        def greet(to_half):
            def act(d):
                pl.semaphore_signal(
                    barrier,
                    inc=1,
                    device_id={"half": to_half, "ctx": peer(d)},
                    device_id_type=pl.DeviceIdType.MESH,
                )

            return act

        params = [
            pltpu.make_async_copy(src.at[:, columns(place)], dst.at[place], p_sem.at[place, i])
            for place in range(2)
            for i, (src, dst) in enumerate(((d_hbm, db), (r_hbm, rb)))
        ]
        for copy in params:
            copy.start()
        for place in range(2):
            for c in range(CHUNKS):
                load(k_hbm, kb, k_sem, place, c).start()
                load(v_hbm, vb, v_sem, place, c).start()
        for place in range(2):
            for c in range(CHUNKS):
                load(q_hbm, qb, q_sem, place, c).start()
        each(1, greet(half))
        each(0, greet(1 - half))

        def reg(place, m):
            return pl.ds(pl.multiple_of((place * modes + m) * SUBS, SUBS), SUBS)

        def row(place, t):
            return pl.ds(pl.multiple_of((place * span + t) * SUBS, SUBS), SUBS)

        def tile(place, t, b):
            return pl.ds((place * span + t) * SUBS + b, SUBS, stride=SUBS)

        for copy in params:
            copy.wait()
        for place in range(2):
            for b in range(SUBS):
                lanes = pl.ds(b * LANES, LANES)
                for m in range(0, modes, SUBS):
                    d = db[place, m : m + SUBS, lanes]
                    r = rb[place, m : m + SUBS, lanes]
                    at = pl.ds((place * modes + m) * SUBS + b, SUBS, stride=SUBS)
                    rate[at, :] = d
                    fade[at, :] = jnp.exp(-d)
                    amp[at, :] = r * jnp.sqrt(d)

        def arrive(place, c):
            load(k_hbm, kb, k_sem, place, c).wait()
            load(v_hbm, vb, v_sem, place, c).wait()

        def spread(place, t, to):
            for b in range(SUBS):
                lanes = pl.ds(b * LANES, LANES)
                x = kb[place, pl.ds(t, STEP), lanes].astype(F32) * vb[place, pl.ds(t, STEP), lanes].astype(F32)
                for j in range(0, STEP, SUBS):
                    xb[tile(place, to + j, b), :] = x[j : j + SUBS]

        zeros = jnp.zeros((SUBS, LANES), F32)

        held = (zeros,) * modes
        for c in range(CHUNKS):
            first = c * chunk
            arrive(0, c)
            spread(0, first, first)

            def gather(i, held, first=first):
                t = pl.multiple_of(first + i * STEP, STEP)
                xs = [xb[row(0, t + j), :] for j in range(STEP)]
                held = list(held)
                for m in range(modes):
                    a = fade[reg(0, m), :]
                    for x in xs:
                        held[m] = held[m] * a + x
                spread(0, pl.multiple_of(jnp.minimum(t + STEP, first + chunk - STEP), STEP), t + STEP)
                return tuple(held)

            held = lax.fori_loop(0, chunk // STEP, gather, held)
        for m in range(modes):
            ends[m] = held[m]

        pl.semaphore_wait(barrier, 2 * ctx_size - 1)
        each(1, lambda d: to_owner(d).start())

        def respond(place, look):
            g = g_ref[pl.ds(pl.multiple_of(owner[place] * SUBS, SUBS), SUBS), :]

            def body(i, held):
                t = pl.multiple_of(i * STEP, STEP)
                held = list(held)
                for s in range(0, STEP, SUBS):
                    xs = [xb[row(place, t + s + j), :] for j in range(SUBS)]
                    ys = [g * x for x in xs]
                    for m in range(modes):
                        a = fade[reg(place, m), :]
                        w = amp[reg(place, m), :]
                        for j in range(SUBS):
                            held[m] = held[m] * a + xs[j]
                            ys[j] = ys[j] + w * held[m]
                    for j in range(SUBS):
                        xb[row(place, t + s + j), :] = ys[j]
                if look:
                    spread(place, pl.multiple_of(jnp.minimum(t + STEP, rows - STEP), STEP), t + STEP)
                return tuple(held)

            lax.fori_loop(0, rows // STEP, body, (zeros,) * modes)

        respond(0, False)

        heard[ctx] = ends[ctx]
        each(1, lambda d: to_owner(d).wait())
        whole = jnp.exp(-float(rows) * rate[reg(0, ctx), :])
        state = zeros
        for j in range(ctx_size):
            starts[j] = state
            state = state * whole + heard[j]
        each(1, lambda d: to_same(d).start())
        each(0, lambda d: to_twin(d).start())

        for c in range(CHUNKS):
            arrive(1, c)
        spread(1, 0, 0)
        respond(1, True)

        enter[0, ctx] = starts[ctx]
        each(1, lambda d: to_same(d).wait())
        each(0, lambda d: to_twin(d).wait())

        for place in range(2):
            state = tuple(amp[reg(place, m), :] * enter[place, m] for m in range(modes))
            for c in range(CHUNKS):
                load(q_hbm, qb, q_sem, place, c).wait()

                def finish(i, state, place=place, first=c * chunk):
                    t = pl.multiple_of(first + i * STEP, STEP)
                    state = list(state)
                    for s in range(0, STEP, SUBS):
                        ys = [xb[row(place, t + s + j), :] for j in range(SUBS)]
                        for m in range(modes):
                            a = fade[reg(place, m), :]
                            for j in range(SUBS):
                                state[m] = state[m] * a
                                ys[j] = ys[j] + state[m]
                        for j in range(SUBS):
                            xb[row(place, t + s + j), :] = ys[j]
                    for b in range(SUBS):
                        lanes = pl.ds(b * LANES, LANES)
                        y = jnp.concatenate([xb[tile(place, t + j, b), :] for j in range(0, STEP, SUBS)])
                        gate = qb[place, pl.ds(t, STEP), lanes].astype(F32)
                        ob[place, pl.ds(t, STEP), lanes] = (gate * y).astype(jnp.bfloat16)
                    return tuple(state)

                state = lax.fori_loop(0, chunk // STEP, finish, state)
                store(place, c).start()
        for place in range(2):
            for c in range(CHUNKS):
                store(place, c).wait()

    return kernel


def shards(query_gate, key_gate, value_input, residues, decays, skip_gain):
    rows, width = key_gate.shape
    modes = residues.shape[0]
    group = width // 2
    ctx_size = lax.axis_size("ctx")
    assert group == SUBS * LANES and modes == ctx_size
    wide = (2, rows, group)
    register = (SUBS, LANES)
    dma = pltpu.SemaphoreType.DMA
    anywhere = pl.BlockSpec(memory_space=pl.ANY)
    return pl.pallas_call(
        make_kernel(rows, group, modes, ctx_size),
        out_shape=jax.ShapeDtypeStruct((rows, width), jnp.bfloat16),
        in_specs=[anywhere] * 5 + [pl.BlockSpec(memory_space=pltpu.VMEM)],
        out_specs=anywhere,
        scratch_shapes=[
            pltpu.VMEM(wide, jnp.bfloat16),
            pltpu.VMEM(wide, jnp.bfloat16),
            pltpu.VMEM(wide, jnp.bfloat16),
            pltpu.VMEM(wide, jnp.bfloat16),
            pltpu.VMEM((2, modes, group), F32),
            pltpu.VMEM((2, modes, group), F32),
            pltpu.VMEM((2 * (rows + STEP) * SUBS, LANES), F32),
            pltpu.VMEM((2 * modes * SUBS, LANES), F32),
            pltpu.VMEM((2 * modes * SUBS, LANES), F32),
            pltpu.VMEM((2 * modes * SUBS, LANES), F32),
            pltpu.VMEM((modes, *register), F32),
            pltpu.VMEM((ctx_size, *register), F32),
            pltpu.VMEM((ctx_size, *register), F32),
            pltpu.VMEM((2, modes, *register), F32),
            dma((2, 2)),
            dma((2, CHUNKS)),
            dma((2, CHUNKS)),
            dma((2, CHUNKS)),
            dma((2, CHUNKS)),
        ]
        + [dma((ctx_size,))] * 6,
        compiler_params=pltpu.CompilerParams(
            collective_id=0, has_side_effects=True, vmem_limit_bytes=48 << 20
        ),
    )(query_gate, key_gate, value_input, residues, decays, skip_gain.reshape(2 * SUBS, LANES))


def solution(mesh):
    placed = (
        P("ctx", "chan"),
        P("ctx", "chan"),
        P("ctx", "chan"),
        P(None, "chan"),
        P(None, "chan"),
        P("chan"),
    )
    return jax.shard_map(shards, mesh=mesh, in_specs=placed, out_specs=P("ctx", "chan"), check_vma=False)
```

```python
import jax
import jax.numpy as jnp
from jax import lax
from jax.experimental import pallas as pl
from jax.experimental.pallas import tpu as pltpu
from jax.sharding import PartitionSpec as P

F32 = jnp.float32
LANES = 128
SUBS = 8
TILE = 16
BLOCK = 8
STEP = 32
CHUNKS = 4
SIDE = 4


def torus(d):
    return sum(min(c, SIDE - c) for c in d)


OFFSETS = sorted(((a, b) for a in range(SIDE) for b in range(SIDE)), key=torus, reverse=True)
BACK = [OFFSETS.index((-a % SIDE, -b % SIDE)) for a, b in OFFSETS]
MODES = len(OFFSETS)
FAR = [n for n in range(MODES) if torus(OFFSETS[n]) > 2]
MID = [n for n in range(MODES) if torus(OFFSETS[n]) == 2]
NEAR = [n for n in range(MODES) if torus(OFFSETS[n]) < 2]
SELF = MODES - 1


def make_kernel(rows, group):
    chunk = rows // CHUNKS
    span = rows + STEP

    def kernel(
        q_hbm, k_hbm, v_hbm, r_hbm, d_hbm, g_hbm, o_hbm,
        kb, vb, qb, ob, rb, db, gb, xb, rate, raw, fade, fade8, amp, taps, left, ends, heard, starts, enter,
        p_sem, k_sem, v_sem, q_sem, o_sem, e_send, e_recv, s_send, s_recv, t_send, t_recv,
    ):
        half = lax.axis_index("half")
        ctx = lax.axis_index("ctx")
        owner = (half, 1 - half)

        def columns(place):
            return pl.ds(pl.multiple_of(owner[place] * group, group), group)

        def load(hbm, buf, sem, place, c):
            at = pl.ds(c * chunk, chunk)
            return pltpu.make_async_copy(hbm.at[at, columns(place)], buf.at[place, at, :], sem.at[place, c])

        def store(place, c):
            at = pl.ds(c * chunk, chunk)
            return pltpu.make_async_copy(ob.at[place, at, :], o_hbm.at[at, columns(place)], o_sem.at[place, c])

        def remote(src, dst, send_sem, recv_sem, to_half, to_ctx):
            return pltpu.make_async_remote_copy(
                src_ref=src,
                dst_ref=dst,
                send_sem=send_sem,
                recv_sem=recv_sem,
                device_id={"half": to_half, "ctx": to_ctx},
                device_id_type=pl.DeviceIdType.MESH,
            )

        def peer(n):
            a, b = OFFSETS[n]
            return lax.rem(ctx // SIDE + a, SIDE) * SIDE + lax.rem(lax.rem(ctx, SIDE) + b, SIDE)

        def to_owner(n):
            return remote(ends.at[n], heard.at[ctx], e_send.at[n], e_recv.at[n], half, peer(n))

        def to_same(n):
            return remote(starts.at[peer(n)], enter.at[0, BACK[n]], s_send.at[n], s_recv.at[n], half, peer(n))

        def to_twin(n):
            return remote(starts.at[peer(n)], enter.at[1, BACK[n]], t_send.at[n], t_recv.at[n], 1 - half, peer(n))

        barrier = pltpu.get_barrier_semaphore()

        def greet(to_half, to_ctx):
            pl.semaphore_signal(
                barrier, inc=1, device_id={"half": to_half, "ctx": to_ctx}, device_id_type=pl.DeviceIdType.MESH
            )

        params = [
            pltpu.make_async_copy(src.at[:, columns(place)], dst.at[place], p_sem.at[place, i])
            for place in range(2)
            for i, (src, dst) in enumerate(((d_hbm, db), (r_hbm, rb)))
        ]
        params += [
            pltpu.make_async_copy(
                g_hbm.at[pl.ds(pl.multiple_of(owner[place] * SUBS, SUBS), SUBS), :], gb.at[place], p_sem.at[place, 2]
            )
            for place in range(2)
        ]
        for copy in params:
            copy.start()
        for place in range(2):
            for c in range(CHUNKS):
                load(k_hbm, kb, k_sem, place, c).start()
                load(v_hbm, vb, v_sem, place, c).start()
        for place in range(2):
            for c in range(CHUNKS):
                load(q_hbm, qb, q_sem, place, c).start()
        for n in range(MODES):
            if n != SELF:
                greet(half, peer(n))
            greet(1 - half, peer(n))

        def reg(place, n):
            return pl.ds(pl.multiple_of((place * MODES + n) * SUBS, SUBS), SUBS)

        def row(place, t):
            return pl.ds(pl.multiple_of((place * span + t) * SUBS, SUBS), SUBS)

        def tile(place, t, b):
            return pl.ds((place * span + t) * SUBS + b, SUBS, stride=SUBS)

        for copy in params:
            copy.wait()
        for place in range(2):
            for b in range(SUBS):
                lanes = pl.ds(b * LANES, LANES)
                for m in range(0, MODES, SUBS):
                    at = pl.ds((place * MODES + m) * SUBS + b, SUBS, stride=SUBS)
                    rate[at, :] = db[place, m : m + SUBS, lanes]
                    raw[at, :] = rb[place, m : m + SUBS, lanes]
        for place in range(2):
            for n in range(MODES):
                d = rate[reg(place, peer(n)), :]
                a = jnp.exp(-d)
                fade[reg(place, n), :] = a
                fade8[reg(place, n), :] = jnp.exp(-float(BLOCK) * d)
                amp[reg(place, n), :] = raw[reg(place, peer(n)), :] * jnp.sqrt(d)

        def make_taps(place):
            terms = [amp[reg(place, n), :] for n in range(MODES)]
            for j in range(BLOCK):
                total = sum(terms[1:], terms[0])
                taps[reg(place, j), :] = total + gb[place] if j == 0 else total
                terms = [term * fade[reg(place, n), :] for n, term in enumerate(terms)]
            for n in range(MODES):
                amp[reg(place, n), :] = amp[reg(place, n), :] * fade[reg(place, n), :]

        def arrive(place, c):
            load(k_hbm, kb, k_sem, place, c).wait()
            load(v_hbm, vb, v_sem, place, c).wait()

        def spread(place, t, to):
            for b in range(SUBS):
                lanes = pl.ds(b * LANES, LANES)
                for i in range(0, STEP, TILE):
                    at = pl.ds(t + i, TILE)
                    x = kb[place, at, lanes].astype(F32) * vb[place, at, lanes].astype(F32)
                    for j in range(0, TILE, SUBS):
                        xb[tile(place, to + i + j, b), :] = x[j : j + SUBS]

        def read(place, t):
            return [xb[row(place, t + j), :] for j in range(BLOCK)]

        def leave(xs, a):
            held = xs[0]
            for x in xs[1:]:
                held = held * a + x
            return held

        def answer(place, t, xs):
            for j in reversed(range(BLOCK)):
                y = taps[reg(place, 0), :] * xs[j]
                for i in range(j):
                    y = y + taps[reg(place, j - i), :] * xs[i]
                xb[row(place, t + j), :] = y

        def gather(slots, look, first, size, held):
            def body(i, held):
                t = pl.multiple_of(first + i * STEP, STEP)
                held = list(held)
                for s in range(0, STEP, BLOCK):
                    xs = read(0, t + s)
                    for at, n in enumerate(slots):
                        e = leave(xs, fade[reg(0, n), :])
                        left[0, (t + s) // BLOCK, n] = e
                        held[at] = held[at] * fade8[reg(0, n), :] + e
                if look:
                    spread(0, pl.multiple_of(jnp.minimum(t + STEP, first + size - STEP), STEP), t + STEP)
                return tuple(held)

            return lax.fori_loop(0, size // STEP, body, held)

        zeros = jnp.zeros((SUBS, LANES), F32)
        held = (zeros,) * len(FAR)
        for c in range(CHUNKS):
            arrive(0, c)
            spread(0, c * chunk, c * chunk)
            held = gather(FAR, True, c * chunk, chunk, held)
        for at, n in enumerate(FAR):
            ends[n] = held[at]
        held = gather(MID, False, 0, rows, (zeros,) * len(MID))
        for at, n in enumerate(MID):
            ends[n] = held[at]

        pl.semaphore_wait(barrier, 2 * MODES - 1)
        for n in FAR + MID:
            to_owner(n).start()
        held = gather(NEAR, False, 0, rows, (zeros,) * len(NEAR))
        for at, n in enumerate(NEAR):
            ends[n] = held[at]
        for n in NEAR:
            if n != SELF:
                to_owner(n).start()

        make_taps(0)
        make_taps(1)

        def own(i, carry):
            t = pl.multiple_of(i * STEP, STEP)
            for s in range(0, STEP, BLOCK):
                answer(0, t + s, read(0, t + s))
            return carry

        lax.fori_loop(0, rows // STEP, own, 0)

        def other(i, carry):
            t = pl.multiple_of(i * STEP, STEP)
            for s in range(0, STEP, BLOCK):
                xs = read(1, t + s)
                for n in range(MODES):
                    left[1, (t + s) // BLOCK, n] = leave(xs, fade[reg(1, n), :])
                answer(1, t + s, xs)
            spread(1, pl.multiple_of(jnp.minimum(t + STEP, rows - STEP), STEP), t + STEP)
            return carry

        for c in range(CHUNKS):
            arrive(1, c)
        spread(1, 0, 0)
        part = rows // STEP * 5 // 8
        lax.fori_loop(0, part, other, 0)

        heard[ctx] = ends[SELF]
        for n in range(MODES):
            if n != SELF:
                to_owner(n).wait()
        whole = jnp.exp(-float(rows) * rate[reg(0, ctx), :])
        state = zeros
        for j in range(MODES):
            starts[j] = state
            state = state * whole + heard[j]
        for n in range(MODES):
            if n != SELF:
                to_same(n).start()
            to_twin(n).start()
        enter[0, SELF] = starts[ctx]

        lax.fori_loop(part, rows // STEP, other, 0)

        def pour(place, slots, first, size, last, state):
            def body(i, state):
                t = pl.multiple_of(first + i * STEP, STEP)
                state = list(state)
                for s in range(0, STEP, BLOCK):
                    ys = read(place, t + s)
                    for at, n in enumerate(slots):
                        a = fade[reg(place, n), :]
                        now = state[at] * amp[reg(place, n), :]
                        ys[0] = ys[0] + now
                        for j in range(1, BLOCK):
                            now = now * a
                            ys[j] = ys[j] + now
                        state[at] = state[at] * fade8[reg(place, n), :] + left[place, (t + s) // BLOCK, n]
                    for j in range(BLOCK):
                        xb[row(place, t + s + j), :] = ys[j]
                if last:
                    for b in range(SUBS):
                        lanes = pl.ds(b * LANES, LANES)
                        for i in range(0, STEP, TILE):
                            at = pl.ds(t + i, TILE)
                            y = jnp.concatenate([xb[tile(place, t + i + j, b), :] for j in range(0, TILE, SUBS)])
                            ob[place, at, lanes] = (qb[place, at, lanes].astype(F32) * y).astype(jnp.bfloat16)
                return tuple(state)

            return lax.fori_loop(0, size // STEP, body, state)

        for slots in (NEAR, MID):
            for place in range(2):
                for n in slots:
                    if place == 0 and n != SELF:
                        to_same(BACK[n]).wait()
                    if place == 1:
                        to_twin(BACK[n]).wait()
                pour(place, slots, 0, rows, False, tuple(enter[place, n] for n in slots))
        for place in range(2):
            for n in FAR:
                if place == 0:
                    to_same(BACK[n]).wait()
                else:
                    to_twin(BACK[n]).wait()
            state = tuple(enter[place, n] for n in FAR)
            for c in range(CHUNKS):
                load(q_hbm, qb, q_sem, place, c).wait()
                state = pour(place, FAR, c * chunk, chunk, True, state)
                store(place, c).start()
        for place in range(2):
            for c in range(CHUNKS):
                store(place, c).wait()

    return kernel


def shards(query_gate, key_gate, value_input, residues, decays, skip_gain):
    rows, width = key_gate.shape
    group = width // 2
    assert group == SUBS * LANES and residues.shape[0] == MODES == lax.axis_size("ctx")
    wide = (2, rows, group)
    register = (SUBS, LANES)
    dma = pltpu.SemaphoreType.DMA
    hbm = pl.BlockSpec(memory_space=pltpu.HBM)
    return pl.pallas_call(
        make_kernel(rows, group),
        out_shape=jax.ShapeDtypeStruct((rows, width), jnp.bfloat16),
        in_specs=[hbm] * 6,
        out_specs=hbm,
        scratch_shapes=[pltpu.VMEM(wide, jnp.bfloat16)] * 4
        + [pltpu.VMEM((2, MODES, group), F32)] * 2
        + [
            pltpu.VMEM((2, *register), F32),
            pltpu.VMEM((2 * (rows + STEP) * SUBS, LANES), F32),
        ]
        + [pltpu.VMEM((2 * MODES * SUBS, LANES), F32)] * 6
        + [pltpu.VMEM((2, rows // BLOCK, MODES, *register), F32)]
        + [pltpu.VMEM((MODES, *register), F32)] * 3
        + [
            pltpu.VMEM((2, MODES, *register), F32),
            dma((2, 3)),
        ]
        + [dma((2, CHUNKS))] * 4
        + [dma((MODES,))] * 6,
        compiler_params=pltpu.CompilerParams(
            collective_id=0, has_side_effects=True, vmem_limit_bytes=67_043_328
        ),
    )(query_gate, key_gate, value_input, residues, decays, skip_gain.reshape(2 * SUBS, LANES))


def solution(mesh):
    placed = (
        P("ctx", "chan"),
        P("ctx", "chan"),
        P("ctx", "chan"),
        P(None, "chan"),
        P(None, "chan"),
        P("chan"),
    )
    return jax.shard_map(shards, mesh=mesh, in_specs=placed, out_specs=P("ctx", "chan"), check_vma=False)
```

```python
import jax
import jax.numpy as jnp
from jax import lax
from jax.experimental import pallas as pl
from jax.experimental.pallas import tpu as pltpu
from jax.sharding import PartitionSpec as P

F32 = jnp.float32
LANES = 128
SUBS = 8
TILE = 16
BLOCK = 8
STEP = 32
SPAN = 512 + STEP
CHUNKS = 4
SIDE = 4


def torus(d):
    return sum(min(c, SIDE - c) for c in d)


OFFSETS = sorted(((a, b) for a in range(SIDE) for b in range(SIDE)), key=torus, reverse=True)
BACK = [OFFSETS.index((-a % SIDE, -b % SIDE)) for a, b in OFFSETS]
MODES = len(OFFSETS)
FAR = [n for n in range(MODES) if torus(OFFSETS[n]) > 2]
MID = [n for n in range(MODES) if torus(OFFSETS[n]) == 2]
NEAR = [n for n in range(MODES) if torus(OFFSETS[n]) < 2]
SELF = MODES - 1


def reg(place, n):
    return pl.ds(pl.multiple_of((place * MODES + n) * SUBS, SUBS), SUBS)


def row(place, t):
    return pl.ds(pl.multiple_of((place * SPAN + t) * SUBS, SUBS), SUBS)


def tile(place, t, b):
    return pl.ds((place * SPAN + t) * SUBS + b, SUBS, stride=SUBS)


def pour(place, slots, first, size, refs, state, then=None):
    xb, left, fade, fade8, amp = refs

    def body(i, state):
        t = pl.multiple_of(first + i * STEP, STEP)
        state = list(state)
        for s in range(0, STEP, BLOCK):
            ys = [xb[row(place, t + s + j), :] for j in range(BLOCK)]
            for at, n in enumerate(slots):
                a = fade[reg(place, n), :]
                now = state[at] * amp[reg(place, n), :]
                ys[0] = ys[0] + now
                for j in range(1, BLOCK):
                    now = now * a
                    ys[j] = ys[j] + now
                state[at] = state[at] * fade8[reg(place, n), :] + left[place, (t + s) // BLOCK, n]
            for j in range(BLOCK):
                xb[row(place, t + s + j), :] = ys[j]
        if then is not None:
            then(t)
        return tuple(state)

    return lax.fori_loop(0, size // STEP, body, state)


FIRST_VMEM = 40 << 20
SECOND_VMEM = 40 << 20


def make_first(rows, group):
    chunk = rows // CHUNKS
    assert SPAN == rows + STEP

    def kernel(
        k_hbm, v_hbm, r_hbm, d_hbm, g_hbm, xb, left, enter, fade, fade8, amp,
        kb, vb, rb, db, gb, rate, raw, taps, ends, heard, starts,
        p_sem, k_sem, v_sem, e_send, e_recv, s_send, s_recv, t_send, t_recv,
    ):
        half = lax.axis_index("half")
        ctx = lax.axis_index("ctx")
        owner = (half, 1 - half)

        def columns(place):
            return pl.ds(pl.multiple_of(owner[place] * group, group), group)

        def load(hbm, buf, sem, place, c):
            at = pl.ds(c * chunk, chunk)
            return pltpu.make_async_copy(hbm.at[at, columns(place)], buf.at[place, at, :], sem.at[place, c])

        def remote(src, dst, send_sem, recv_sem, to_half, to_ctx):
            return pltpu.make_async_remote_copy(
                src_ref=src,
                dst_ref=dst,
                send_sem=send_sem,
                recv_sem=recv_sem,
                device_id={"half": to_half, "ctx": to_ctx},
                device_id_type=pl.DeviceIdType.MESH,
            )

        def peer(n):
            a, b = OFFSETS[n]
            return lax.rem(ctx // SIDE + a, SIDE) * SIDE + lax.rem(lax.rem(ctx, SIDE) + b, SIDE)

        def to_owner(n):
            return remote(ends.at[n], heard.at[ctx], e_send.at[n], e_recv.at[n], half, peer(n))

        def to_same(n):
            return remote(starts.at[peer(n)], enter.at[0, BACK[n]], s_send.at[n], s_recv.at[n], half, peer(n))

        def to_twin(n):
            return remote(starts.at[peer(n)], enter.at[1, BACK[n]], t_send.at[n], t_recv.at[n], 1 - half, peer(n))

        barrier = pltpu.get_barrier_semaphore()

        def greet(to_half, to_ctx):
            pl.semaphore_signal(
                barrier, inc=1, device_id={"half": to_half, "ctx": to_ctx}, device_id_type=pl.DeviceIdType.MESH
            )

        params = [
            pltpu.make_async_copy(src.at[:, columns(place)], dst.at[place], p_sem.at[place, i])
            for place in range(2)
            for i, (src, dst) in enumerate(((d_hbm, db), (r_hbm, rb)))
        ]
        params += [
            pltpu.make_async_copy(
                g_hbm.at[pl.ds(pl.multiple_of(owner[place] * SUBS, SUBS), SUBS), :], gb.at[place], p_sem.at[place, 2]
            )
            for place in range(2)
        ]
        for copy in params:
            copy.start()
        for place in range(2):
            for c in range(CHUNKS):
                load(k_hbm, kb, k_sem, place, c).start()
                load(v_hbm, vb, v_sem, place, c).start()
        for n in range(MODES):
            if n != SELF:
                greet(half, peer(n))
            greet(1 - half, peer(n))

        for copy in params:
            copy.wait()
        for place in range(2):
            for b in range(SUBS):
                lanes = pl.ds(b * LANES, LANES)
                for m in range(0, MODES, SUBS):
                    at = pl.ds((place * MODES + m) * SUBS + b, SUBS, stride=SUBS)
                    rate[at, :] = db[place, m : m + SUBS, lanes]
                    raw[at, :] = rb[place, m : m + SUBS, lanes]
        for place in range(2):
            for n in range(MODES):
                d = rate[reg(place, peer(n)), :]
                a = jnp.exp(-d)
                fade[reg(place, n), :] = a
                fade8[reg(place, n), :] = jnp.exp(-float(BLOCK) * d)
                amp[reg(place, n), :] = raw[reg(place, peer(n)), :] * jnp.sqrt(d)

        def make_taps(place):
            terms = [amp[reg(place, n), :] for n in range(MODES)]
            for j in range(BLOCK):
                total = sum(terms[1:], terms[0])
                taps[reg(place, j), :] = total + gb[place] if j == 0 else total
                terms = [term * fade[reg(place, n), :] for n, term in enumerate(terms)]
            for n in range(MODES):
                amp[reg(place, n), :] = amp[reg(place, n), :] * fade[reg(place, n), :]

        def arrive(place, c):
            load(k_hbm, kb, k_sem, place, c).wait()
            load(v_hbm, vb, v_sem, place, c).wait()

        def spread(place, t, to):
            for b in range(SUBS):
                lanes = pl.ds(b * LANES, LANES)
                for i in range(0, STEP, TILE):
                    at = pl.ds(t + i, TILE)
                    x = kb[place, at, lanes].astype(F32) * vb[place, at, lanes].astype(F32)
                    for j in range(0, TILE, SUBS):
                        xb[tile(place, to + i + j, b), :] = x[j : j + SUBS]

        def read(place, t):
            return [xb[row(place, t + j), :] for j in range(BLOCK)]

        def leave(xs, a):
            held = xs[0]
            for x in xs[1:]:
                held = held * a + x
            return held

        def answer(place, t, xs):
            for j in reversed(range(BLOCK)):
                y = taps[reg(place, 0), :] * xs[j]
                for i in range(j):
                    y = y + taps[reg(place, j - i), :] * xs[i]
                xb[row(place, t + j), :] = y

        def gather(slots, look, first, size, held):
            def body(i, held):
                t = pl.multiple_of(first + i * STEP, STEP)
                held = list(held)
                for s in range(0, STEP, BLOCK):
                    xs = read(0, t + s)
                    for at, n in enumerate(slots):
                        e = leave(xs, fade[reg(0, n), :])
                        left[0, (t + s) // BLOCK, n] = e
                        held[at] = held[at] * fade8[reg(0, n), :] + e
                if look:
                    spread(0, pl.multiple_of(jnp.minimum(t + STEP, first + size - STEP), STEP), t + STEP)
                return tuple(held)

            return lax.fori_loop(0, size // STEP, body, held)

        zeros = jnp.zeros((SUBS, LANES), F32)
        held = (zeros,) * len(FAR)
        for c in range(CHUNKS):
            arrive(0, c)
            spread(0, c * chunk, c * chunk)
            held = gather(FAR, True, c * chunk, chunk, held)
        for at, n in enumerate(FAR):
            ends[n] = held[at]
        held = gather(MID, False, 0, rows, (zeros,) * len(MID))
        for at, n in enumerate(MID):
            ends[n] = held[at]

        pl.semaphore_wait(barrier, 2 * MODES - 1)
        for n in FAR + MID:
            to_owner(n).start()
        held = gather(NEAR, False, 0, rows, (zeros,) * len(NEAR))
        for at, n in enumerate(NEAR):
            ends[n] = held[at]
        for n in NEAR:
            if n != SELF:
                to_owner(n).start()

        make_taps(0)
        make_taps(1)

        def own(i, carry):
            t = pl.multiple_of(i * STEP, STEP)
            for s in range(0, STEP, BLOCK):
                answer(0, t + s, read(0, t + s))
            return carry

        lax.fori_loop(0, rows // STEP, own, 0)

        def other(i, carry):
            t = pl.multiple_of(i * STEP, STEP)
            for s in range(0, STEP, BLOCK):
                xs = read(1, t + s)
                for n in range(MODES):
                    left[1, (t + s) // BLOCK, n] = leave(xs, fade[reg(1, n), :])
                answer(1, t + s, xs)
            spread(1, pl.multiple_of(jnp.minimum(t + STEP, rows - STEP), STEP), t + STEP)
            return carry

        for c in range(CHUNKS):
            arrive(1, c)
        spread(1, 0, 0)
        part = rows // STEP * 5 // 8
        lax.fori_loop(0, part, other, 0)

        heard[ctx] = ends[SELF]
        for n in range(MODES):
            if n != SELF:
                to_owner(n).wait()
        whole = jnp.exp(-float(rows) * rate[reg(0, ctx), :])
        state = zeros
        for j in range(MODES):
            starts[j] = state
            state = state * whole + heard[j]
        for n in range(MODES):
            if n != SELF:
                to_same(n).start()
            to_twin(n).start()
        enter[0, SELF] = starts[ctx]

        lax.fori_loop(part, rows // STEP, other, 0)

        for slots in (NEAR, MID):
            for place in range(2):
                for n in slots:
                    if place == 0 and n != SELF:
                        to_same(BACK[n]).wait()
                    if place == 1:
                        to_twin(BACK[n]).wait()
                state = tuple(enter[place, n] for n in slots)
                pour(place, slots, 0, rows, (xb, left, fade, fade8, amp), state)
        for n in FAR:
            to_same(BACK[n]).wait()
            to_twin(BACK[n]).wait()

    return kernel


def finish(place, first, size, state, refs, qb, ob):
    xs, xb, left, fade, fade8, amp = refs

    def body(i, state):
        t = pl.multiple_of(first + i * STEP, STEP)
        state = list(state)
        for s in range(0, STEP, BLOCK):
            ys = [xs[row(place, t + s + j), :] for j in range(BLOCK)]
            for at, n in enumerate(FAR):
                a = fade[reg(place, n), :]
                now = state[at] * amp[reg(place, n), :]
                ys[0] = ys[0] + now
                for j in range(1, BLOCK):
                    now = now * a
                    ys[j] = ys[j] + now
                state[at] = state[at] * fade8[reg(place, n), :] + left[place, (t + s) // BLOCK, n]
            for j in range(BLOCK):
                xb[pl.ds((s + j) * SUBS, SUBS), :] = ys[j]
        for b in range(SUBS):
            lanes = pl.ds(b * LANES, LANES)
            for i in range(0, STEP, TILE):
                at = pl.ds(t + i, TILE)
                y = jnp.concatenate(
                    [xb[pl.ds((i + j) * SUBS + b, SUBS, stride=SUBS), :] for j in range(0, TILE, SUBS)]
                )
                ob[place, at, lanes] = (qb[place, at, lanes].astype(F32) * y).astype(jnp.bfloat16)
        return tuple(state)

    return lax.fori_loop(0, size // STEP, body, state)


def make_second(rows, group):
    chunk = rows // CHUNKS

    def kernel(q_hbm, xs, left, enter, fade, fade8, amp, o_hbm, xb, qb, ob, q_sem, o_sem):
        half = lax.axis_index("half")
        owner = (half, 1 - half)

        def columns(place):
            return pl.ds(pl.multiple_of(owner[place] * group, group), group)

        def load(place, c):
            at = pl.ds(c * chunk, chunk)
            return pltpu.make_async_copy(q_hbm.at[at, columns(place)], qb.at[place, at, :], q_sem.at[place, c])

        def store(place, c):
            at = pl.ds(c * chunk, chunk)
            return pltpu.make_async_copy(ob.at[place, at, :], o_hbm.at[at, columns(place)], o_sem.at[place, c])

        for place in range(2):
            for c in range(CHUNKS):
                load(place, c).start()
        for place in range(2):
            state = tuple(enter[place, n] for n in FAR)
            for c in range(CHUNKS):
                load(place, c).wait()
                state = finish(place, c * chunk, chunk, state, (xs, xb, left, fade, fade8, amp), qb, ob)
                store(place, c).start()
        for place in range(2):
            for c in range(CHUNKS):
                store(place, c).wait()

    return kernel


def shards(query_gate, key_gate, value_input, residues, decays, skip_gain):
    rows, width = key_gate.shape
    group = width // 2
    assert group == SUBS * LANES and residues.shape[0] == MODES == lax.axis_size("ctx")
    wide = (2, rows, group)
    register = (SUBS, LANES)
    dma = pltpu.SemaphoreType.DMA
    hbm = pl.BlockSpec(memory_space=pltpu.HBM)
    vmem = pl.BlockSpec(memory_space=pltpu.VMEM)
    table = (2 * MODES * SUBS, LANES)
    between = [
        (2 * SPAN * SUBS, LANES),
        (2, rows // BLOCK, MODES, *register),
        (2, MODES, *register),
        table,
        table,
        table,
    ]
    kept = pl.pallas_call(
        make_first(rows, group),
        out_shape=[jax.ShapeDtypeStruct(shape, F32) for shape in between],
        in_specs=[hbm] * 5,
        out_specs=[vmem] * len(between),
        scratch_shapes=[pltpu.VMEM(wide, jnp.bfloat16)] * 2
        + [pltpu.VMEM((2, MODES, group), F32)] * 2
        + [pltpu.VMEM((2, *register), F32)]
        + [pltpu.VMEM(table, F32)] * 3
        + [pltpu.VMEM((MODES, *register), F32)] * 3
        + [dma((2, 3))]
        + [dma((2, CHUNKS))] * 2
        + [dma((MODES,))] * 6,
        compiler_params=pltpu.CompilerParams(
            collective_id=0, has_side_effects=True, vmem_limit_bytes=FIRST_VMEM
        ),
    )(*(pltpu.with_memory_space_constraint(x, pltpu.HBM) for x in (key_gate, value_input, residues, decays, skip_gain.reshape(2 * SUBS, LANES))))
    return pl.pallas_call(
        make_second(rows, group),
        out_shape=jax.ShapeDtypeStruct((rows, width), jnp.bfloat16),
        in_specs=[hbm] + [vmem] * len(between),
        out_specs=hbm,
        scratch_shapes=[pltpu.VMEM((STEP * SUBS, LANES), F32)]
        + [pltpu.VMEM(wide, jnp.bfloat16)] * 2
        + [dma((2, CHUNKS))] * 2,
        compiler_params=pltpu.CompilerParams(vmem_limit_bytes=SECOND_VMEM),
    )(pltpu.with_memory_space_constraint(query_gate, pltpu.HBM), *kept)


def solution(mesh):
    placed = (
        P("ctx", "chan"),
        P("ctx", "chan"),
        P("ctx", "chan"),
        P(None, "chan"),
        P(None, "chan"),
        P("chan"),
    )
    return jax.shard_map(shards, mesh=mesh, in_specs=placed, out_specs=P("ctx", "chan"), check_vma=False)
```

```python
import jax
import jax.numpy as jnp
from jax import lax
from jax.experimental import pallas as pl
from jax.experimental.pallas import tpu as pltpu
from jax.sharding import PartitionSpec as P

F32 = jnp.float32
LANES = 128
SUBS = 8
TILE = 16
BLOCK = 8
STEP = 32
ROWS = 512
SPAN = ROWS + STEP
CHUNKS = 4
SIDE = 4
MODES = 16
OWNED = MODES // SIDE
AWAY = (1, 3, 2, 0)
BACK = tuple(AWAY.index(-a % SIDE) for a in AWAY)
SELF = SIDE - 1
FIRST_VMEM = 36 << 20
SECOND_VMEM = 36 << 20


def reg(place, n):
    return pl.ds(pl.multiple_of((place * MODES + n) * SUBS, SUBS), SUBS)


def row(place, t):
    return pl.ds(pl.multiple_of((place * SPAN + t) * SUBS, SUBS), SUBS)


def tile(place, t, b):
    return pl.ds((place * SPAN + t) * SUBS + b, SUBS, stride=SUBS)


def first_kernel(
    q_hbm, k_hbm, v_hbm, r_hbm, d_hbm, g_hbm, xb, enter, fade, amp, qb,
    kb, vb, rb, db, gb, rate, raw, fade8, lead, taps, left, ends, heard, sums, earlier, before, starts,
    p_sem, k_sem, v_sem, q_sem, a_send, a_recv, b_send, b_recv, c_send, c_recv, t_send, t_recv,
):
    group = SUBS * LANES
    chunk = ROWS // CHUNKS
    half = lax.axis_index("half")
    ctx = lax.axis_index("ctx")
    z = ctx // SIDE
    y = lax.rem(ctx, SIDE)
    owner = (half, 1 - half)

    def columns(place):
        return pl.ds(pl.multiple_of(owner[place] * group, group), group)

    def load(hbm, buf, sem, place, c):
        at = pl.ds(c * chunk, chunk)
        return pltpu.make_async_copy(hbm.at[at, columns(place)], buf.at[place, at, :], sem.at[place, c])

    def remote(src, dst, send_sem, recv_sem, to_half, to_z, to_y):
        return pltpu.make_async_remote_copy(
            src_ref=src,
            dst_ref=dst,
            send_sem=send_sem,
            recv_sem=recv_sem,
            device_id={"half": to_half, "ctx": to_z * SIDE + to_y},
            device_id_type=pl.DeviceIdType.MESH,
        )

    def along(k):
        return lax.rem(y + AWAY[k], SIDE)

    def to_owner(k):
        return remote(
            ends.at[pl.ds(k * OWNED, OWNED)], heard.at[y], a_send.at[k], a_recv.at[k], half, z, along(k)
        )

    def to_later(dz):
        return remote(sums, earlier.at[z], b_send.at[dz - 1], b_recv.at[dz - 1], half, lax.rem(z + dz, SIDE), y)

    def to_same(k):
        return remote(
            starts.at[along(k)], enter.at[0, pl.ds(BACK[k] * OWNED, OWNED)], c_send.at[k], c_recv.at[k], half, z, along(k)
        )

    def to_twin(k):
        return remote(
            starts.at[along(k)], enter.at[1, pl.ds(BACK[k] * OWNED, OWNED)], t_send.at[k], t_recv.at[k], 1 - half, z, along(k)
        )

    barrier = pltpu.get_barrier_semaphore()

    def greet(to_half, to_z, to_y):
        pl.semaphore_signal(
            barrier,
            inc=1,
            device_id={"half": to_half, "ctx": to_z * SIDE + to_y},
            device_id_type=pl.DeviceIdType.MESH,
        )

    rates = [pltpu.make_async_copy(d_hbm.at[:, columns(p)], db.at[p], p_sem.at[p, 0]) for p in range(2)]
    others = [pltpu.make_async_copy(r_hbm.at[:, columns(p)], rb.at[p], p_sem.at[p, 1]) for p in range(2)]
    others += [
        pltpu.make_async_copy(
            g_hbm.at[pl.ds(pl.multiple_of(owner[p] * SUBS, SUBS), SUBS), :], gb.at[p], p_sem.at[p, 2]
        )
        for p in range(2)
    ]
    rates[0].start()
    for c in range(CHUNKS):
        load(k_hbm, kb, k_sem, 0, c).start()
        load(v_hbm, vb, v_sem, 0, c).start()
    for k in range(SIDE):
        if k != SELF:
            greet(half, z, along(k))
        greet(1 - half, z, along(k))
    for dz in range(1, SIDE):
        greet(half, lax.rem(z + dz, SIDE), y)
    rates[1].start()
    for copy in others:
        copy.start()
    for c in range(CHUNKS):
        load(k_hbm, kb, k_sem, 1, c).start()
        load(v_hbm, vb, v_sem, 1, c).start()
    for p in range(2):
        for c in range(CHUNKS):
            load(q_hbm, qb, q_sem, p, c).start()

    def turn(src, dst, place):
        for b in range(SUBS):
            lanes = pl.ds(b * LANES, LANES)
            for m in range(0, MODES, SUBS):
                at = pl.ds((place * MODES + m) * SUBS + b, SUBS, stride=SUBS)
                dst[at, :] = src[place, m : m + SUBS, lanes]

    modes = [along(k) * OWNED + e for k in range(SIDE) for e in range(OWNED)]

    def decays(place):
        for n, m in enumerate(modes):
            fade[reg(place, n), :] = jnp.exp(-rate[reg(place, m), :])

    rates[0].wait()
    turn(db, rate, 0)
    decays(0)
    for n, m in enumerate(modes):
        fade8[reg(0, n), :] = jnp.exp(-float(BLOCK) * rate[reg(0, m), :])

    def arrive(place, c):
        load(k_hbm, kb, k_sem, place, c).wait()
        load(v_hbm, vb, v_sem, place, c).wait()

    def spread(place, t, to):
        for b in range(SUBS):
            lanes = pl.ds(b * LANES, LANES)
            for i in range(0, STEP, TILE):
                at = pl.ds(t + i, TILE)
                x = kb[place, at, lanes].astype(F32) * vb[place, at, lanes].astype(F32)
                for j in range(0, TILE, SUBS):
                    xb[tile(place, to + i + j, b), :] = x[j : j + SUBS]

    def read(place, t):
        return [xb[row(place, t + j), :] for j in range(BLOCK)]

    def gather(slots, look, first, size, held):
        def body(i, held):
            t = pl.multiple_of(first + i * STEP, STEP)
            held = list(held)
            for s in range(0, STEP, BLOCK):
                xs = read(0, t + s)
                for at, n in enumerate(slots):
                    a = fade[reg(0, n), :]
                    e = xs[0]
                    for x in xs[1:]:
                        e = e * a + x
                    left[(t + s) // BLOCK, n] = e
                    held[at] = held[at] * fade8[reg(0, n), :] + e
            if look:
                spread(0, pl.multiple_of(jnp.minimum(t + STEP, first + size - STEP), STEP), t + STEP)
            return tuple(held)

        return lax.fori_loop(0, size // STEP, body, held)

    zeros = jnp.zeros((SUBS, LANES), F32)

    def leave(slots, held):
        for at, n in enumerate(slots):
            ends[n] = held[at]

    slots = range(2 * OWNED)
    held = (zeros,) * len(slots)
    for c in range(CHUNKS):
        arrive(0, c)
        spread(0, c * chunk, c * chunk)
        held = gather(slots, True, c * chunk, chunk, held)
    leave(slots, held)
    pl.semaphore_wait(barrier, 3 * SIDE - 2)
    to_owner(0).start()
    to_owner(1).start()
    for k in range(2, SIDE):
        slots = range(k * OWNED, (k + 1) * OWNED)
        leave(slots, gather(slots, False, 0, ROWS, (zeros,) * OWNED))
        if k != SELF:
            to_owner(k).start()
    for e in range(OWNED):
        heard[y, e] = ends[SELF * OWNED + e]

    rates[1].wait()
    turn(db, rate, 1)
    decays(1)
    for copy in others:
        copy.wait()
    for place in range(2):
        turn(rb, raw, place)
        for n, m in enumerate(modes):
            amp[reg(place, n), :] = raw[reg(place, m), :] * jnp.sqrt(rate[reg(place, m), :])
    terms = [amp[reg(0, n), :] for n in range(MODES)]
    for j in range(BLOCK):
        total = sum(terms[1:], terms[0])
        taps[reg(0, j), :] = total + gb[0] if j == 0 else total
        if j < BLOCK - 1:
            terms = [term * fade[reg(0, n), :] for n, term in enumerate(terms)]
        if j == 0:
            for n, term in enumerate(terms):
                lead[reg(0, n), :] = term

    def own(i, state):
        t = pl.multiple_of(i * STEP, STEP)
        state = list(state)
        for s in range(0, STEP, BLOCK):
            xs = read(0, t + s)
            ys = []
            for j in range(BLOCK):
                out = taps[reg(0, 0), :] * xs[j]
                for i in range(j):
                    out = out + taps[reg(0, j - i), :] * xs[i]
                ys.append(out)
            for n in range(MODES):
                a = fade[reg(0, n), :]
                now = state[n] * lead[reg(0, n), :]
                ys[0] = ys[0] + now
                for j in range(1, BLOCK):
                    now = now * a
                    ys[j] = ys[j] + now
                state[n] = state[n] * fade8[reg(0, n), :] + left[(t + s) // BLOCK, n]
            for j in range(BLOCK):
                xb[row(0, t + s + j), :] = ys[j]
        return tuple(state)

    def other(i, held):
        t = pl.multiple_of(i * STEP, STEP)
        held = list(held)
        g = gb[1]
        for s in range(0, STEP, BLOCK):
            xs = read(1, t + s)
            ys = [g * x for x in xs]
            for n in range(MODES):
                a = fade[reg(1, n), :]
                w = amp[reg(1, n), :]
                for j in range(BLOCK):
                    held[n] = held[n] * a + xs[j]
                    ys[j] = ys[j] + w * held[n]
            for j in range(BLOCK):
                xb[row(1, t + s + j), :] = ys[j]
        spread(1, pl.multiple_of(jnp.minimum(t + STEP, ROWS - STEP), STEP), t + STEP)
        return tuple(held)

    steps = ROWS // STEP
    late = jnp.where(y == 0, 2, jnp.where(y == 2, 0, 1))
    part_a = jnp.where(y == 0, steps, jnp.where(y == 2, 5, 11))
    part_b = jnp.where(z == 0, late // 2, jnp.where(z == SIDE - 1, 3 + 4 * late, 4 * late))

    state = lax.fori_loop(0, part_a, own, (zeros,) * MODES)

    for k in range(SIDE):
        if k != SELF:
            to_owner(k).wait()
    for e in range(OWNED):
        whole = jnp.exp(-float(ROWS) * rate[reg(0, y * OWNED + e), :])
        total = zeros
        for place in range(SIDE):
            before[place, e] = total
            total = total * whole + heard[place, e]
        sums[e] = total
    for dz in range(1, SIDE):

        @pl.when(z + dz < SIDE)
        def _(dz=dz):
            to_later(dz).start()

    lax.fori_loop(part_a, steps, own, state)
    for c in range(CHUNKS):
        arrive(1, c)
    spread(1, 0, 0)
    held = lax.fori_loop(0, part_b, other, (zeros,) * MODES)

    for dz in range(1, SIDE):

        @pl.when(z - dz >= 0)
        def _(dz=dz):
            to_later(dz).wait_recv()

    for e in range(OWNED):
        d = rate[reg(0, y * OWNED + e), :]
        row_long = jnp.exp(-float(SIDE * ROWS) * d)
        whole = jnp.exp(-float(ROWS) * d)
        total = lax.fori_loop(0, z, lambda i, total: total * row_long + earlier[i, e], zeros)
        for place in range(SIDE):
            starts[place, e] = total + before[place, e]
            total = total * whole
    for k in range(SIDE):
        if k != SELF:
            to_same(k).start()
        to_twin(k).start()
    for e in range(OWNED):
        enter[0, SELF * OWNED + e] = starts[y, e]

    lax.fori_loop(part_b, steps, other, held)

    for dz in range(1, SIDE):

        @pl.when(z + dz < SIDE)
        def _(dz=dz):
            to_later(dz).wait_send()

    for p in range(2):
        for c in range(CHUNKS):
            load(q_hbm, qb, q_sem, p, c).wait()
    for k in range(SIDE):
        if k != SELF:
            to_same(k).wait()
        to_twin(k).wait()


def second_kernel(xs, enter, fade, amp, qb, o_hbm, xb, ob, o_sem):
    group = SUBS * LANES
    chunk = ROWS // CHUNKS
    half = lax.axis_index("half")
    owner = (half, 1 - half)

    def store(place, c):
        at = pl.ds(c * chunk, chunk)
        columns = pl.ds(pl.multiple_of(owner[place] * group, group), group)
        return pltpu.make_async_copy(ob.at[place, at, :], o_hbm.at[at, columns], o_sem.at[place, c])

    for place in range(2):
        state = tuple(amp[reg(place, n), :] * enter[place, n] for n in range(MODES))
        for c in range(CHUNKS):

            def body(i, state, place=place, first=c * chunk):
                t = pl.multiple_of(first + i * TILE, TILE)
                state = list(state)
                for s in range(0, TILE, BLOCK):
                    ys = [xs[row(place, t + s + j), :] for j in range(BLOCK)]
                    for n in range(MODES):
                        a = fade[reg(place, n), :]
                        for j in range(BLOCK):
                            state[n] = state[n] * a
                            ys[j] = ys[j] + state[n]
                    for j in range(BLOCK):
                        xb[pl.ds((s + j) * SUBS, SUBS), :] = ys[j]
                for b in range(SUBS):
                    lanes = pl.ds(b * LANES, LANES)
                    out = jnp.concatenate([xb[pl.ds(j * SUBS + b, SUBS, stride=SUBS), :] for j in range(0, TILE, SUBS)])
                    gate = qb[place, pl.ds(t, TILE), lanes].astype(F32)
                    ob[place, pl.ds(t, TILE), lanes] = (gate * out).astype(jnp.bfloat16)
                return tuple(state)

            state = lax.fori_loop(0, chunk // TILE, body, state)
            store(place, c).start()
    for place in range(2):
        for c in range(CHUNKS):
            store(place, c).wait()


def shards(query_gate, key_gate, value_input, residues, decays, skip_gain):
    rows, width = key_gate.shape
    group = width // 2
    assert group == SUBS * LANES and rows == ROWS
    assert residues.shape[0] == MODES and lax.axis_size("ctx") == SIDE * SIDE
    wide = pltpu.VMEM((2, rows, group), jnp.bfloat16)
    table = (2 * MODES * SUBS, LANES)
    dma = pltpu.SemaphoreType.DMA
    hbm = pl.BlockSpec(memory_space=pltpu.HBM)
    vmem = pl.BlockSpec(memory_space=pltpu.VMEM)

    def registers(*shape):
        return pltpu.VMEM((*shape, SUBS, LANES), F32)

    operands = (query_gate, key_gate, value_input, residues, decays, skip_gain.reshape(2 * SUBS, LANES))
    kept = pl.pallas_call(
        first_kernel,
        out_shape=[
            jax.ShapeDtypeStruct((2 * SPAN * SUBS, LANES), F32),
            jax.ShapeDtypeStruct((2, MODES, SUBS, LANES), F32),
            jax.ShapeDtypeStruct(table, F32),
            jax.ShapeDtypeStruct(table, F32),
            jax.ShapeDtypeStruct((2, rows, group), jnp.bfloat16),
        ],
        in_specs=[hbm] * 6,
        out_specs=[vmem] * 5,
        scratch_shapes=[wide, wide]
        + [pltpu.VMEM((2, MODES, group), F32)] * 2
        + [registers(2)]
        + [pltpu.VMEM(table, F32)] * 5
        + [
            registers(rows // BLOCK, MODES),
            registers(MODES),
            registers(SIDE, OWNED),
            registers(OWNED),
            registers(SIDE, OWNED),
            registers(SIDE, OWNED),
            registers(SIDE, OWNED),
            dma((2, 3)),
        ]
        + [dma((2, CHUNKS))] * 3
        + [dma((SIDE,))] * 8,
        compiler_params=pltpu.CompilerParams(
            collective_id=0, has_side_effects=True, vmem_limit_bytes=FIRST_VMEM
        ),
    )(*(pltpu.with_memory_space_constraint(x, pltpu.HBM) for x in operands))
    return pl.pallas_call(
        second_kernel,
        out_shape=jax.ShapeDtypeStruct((rows, width), jnp.bfloat16),
        in_specs=[vmem] * 5,
        out_specs=hbm,
        scratch_shapes=[pltpu.VMEM((TILE * SUBS, LANES), F32), wide, dma((2, CHUNKS))],
        compiler_params=pltpu.CompilerParams(vmem_limit_bytes=SECOND_VMEM),
    )(*kept)


def solution(mesh):
    placed = (
        P("ctx", "chan"),
        P("ctx", "chan"),
        P("ctx", "chan"),
        P(None, "chan"),
        P(None, "chan"),
        P("chan"),
    )
    return jax.shard_map(shards, mesh=mesh, in_specs=placed, out_specs=P("ctx", "chan"), check_vma=False)
```

```python
import jax
import jax.numpy as jnp
from jax import lax
from jax.experimental import pallas as pl
from jax.experimental.pallas import tpu as pltpu
from jax.sharding import PartitionSpec as P

F32 = jnp.float32
LANES = 128
SUBS = 8
TILE = 16
BLOCK = 8
STEP = 32
ROWS = 512
SPAN = ROWS + STEP
CHUNKS = 4
SIDE = 4
MODES = 16
OWNED = MODES // SIDE
AWAY = (2, 1, 3, 0)
BACK = tuple(AWAY.index(-a % SIDE) for a in AWAY)
SELF = SIDE - 1
FIRST_VMEM = 36 << 20
SECOND_VMEM = 36 << 20


def reg(place, n):
    return pl.ds(pl.multiple_of((place * MODES + n) * SUBS, SUBS), SUBS)


def row(place, t):
    return pl.ds(pl.multiple_of((place * SPAN + t) * SUBS, SUBS), SUBS)


def tile(place, t, b):
    return pl.ds((place * SPAN + t) * SUBS + b, SUBS, stride=SUBS)


def first_kernel(
    q_hbm, k_hbm, v_hbm, r_hbm, d_hbm, g_hbm, xb, enter, fade, amp, qb,
    kb, vb, rb, db, gb, rate, raw, fade8, lead, taps, left, ends, heard, sums, earlier, before, starts,
    p_sem, k_sem, v_sem, q_sem, a_send, a_recv, b_send, b_recv, c_send, c_recv, t_send, t_recv,
):
    group = SUBS * LANES
    chunk = ROWS // CHUNKS
    half = lax.axis_index("half")
    ctx = lax.axis_index("ctx")
    z = ctx // SIDE
    y = lax.rem(ctx, SIDE)
    owner = (half, 1 - half)

    def columns(place):
        return pl.ds(pl.multiple_of(owner[place] * group, group), group)

    def load(hbm, buf, sem, place, c):
        at = pl.ds(c * chunk, chunk)
        return pltpu.make_async_copy(hbm.at[at, columns(place)], buf.at[place, at, :], sem.at[place, c])

    def remote(src, dst, send_sem, recv_sem, to_half, to_z, to_y):
        return pltpu.make_async_remote_copy(
            src_ref=src,
            dst_ref=dst,
            send_sem=send_sem,
            recv_sem=recv_sem,
            device_id={"half": to_half, "ctx": to_z * SIDE + to_y},
            device_id_type=pl.DeviceIdType.MESH,
        )

    def along(k):
        return lax.rem(y + AWAY[k], SIDE)

    def to_owner(k):
        return remote(
            ends.at[pl.ds(k * OWNED, OWNED)], heard.at[y], a_send.at[k], a_recv.at[k], half, z, along(k)
        )

    def to_later(dz):
        return remote(sums, earlier.at[z], b_send.at[dz - 1], b_recv.at[dz - 1], half, lax.rem(z + dz, SIDE), y)

    def to_same(k):
        return remote(
            starts.at[along(k)], enter.at[0, pl.ds(BACK[k] * OWNED, OWNED)], c_send.at[k], c_recv.at[k], half, z, along(k)
        )

    def to_twin(k):
        return remote(
            starts.at[along(k)], enter.at[1, pl.ds(BACK[k] * OWNED, OWNED)], t_send.at[k], t_recv.at[k], 1 - half, z, along(k)
        )

    barrier = pltpu.get_barrier_semaphore()

    def greet(to_half, to_z, to_y):
        pl.semaphore_signal(
            barrier,
            inc=1,
            device_id={"half": to_half, "ctx": to_z * SIDE + to_y},
            device_id_type=pl.DeviceIdType.MESH,
        )

    rates = [pltpu.make_async_copy(d_hbm.at[:, columns(p)], db.at[p], p_sem.at[p, 0]) for p in range(2)]
    others = [pltpu.make_async_copy(r_hbm.at[:, columns(p)], rb.at[p], p_sem.at[p, 1]) for p in range(2)]
    others += [
        pltpu.make_async_copy(
            g_hbm.at[pl.ds(pl.multiple_of(owner[p] * SUBS, SUBS), SUBS), :], gb.at[p], p_sem.at[p, 2]
        )
        for p in range(2)
    ]
    rates[0].start()
    for c in range(CHUNKS):
        load(k_hbm, kb, k_sem, 0, c).start()
        load(v_hbm, vb, v_sem, 0, c).start()
    for k in range(SIDE):
        if k != SELF:
            greet(half, z, along(k))
        greet(1 - half, z, along(k))
    for dz in range(1, SIDE):
        greet(half, lax.rem(z + dz, SIDE), y)
    rates[1].start()
    for copy in others:
        copy.start()
    for c in range(CHUNKS):
        load(k_hbm, kb, k_sem, 1, c).start()
        load(v_hbm, vb, v_sem, 1, c).start()
    for p in range(2):
        for c in range(CHUNKS):
            load(q_hbm, qb, q_sem, p, c).start()

    def turn(src, dst, place):
        for b in range(SUBS):
            lanes = pl.ds(b * LANES, LANES)
            for m in range(0, MODES, SUBS):
                at = pl.ds((place * MODES + m) * SUBS + b, SUBS, stride=SUBS)
                dst[at, :] = src[place, m : m + SUBS, lanes]

    modes = [along(k) * OWNED + e for k in range(SIDE) for e in range(OWNED)]

    def decays(place):
        for n, m in enumerate(modes):
            fade[reg(place, n), :] = jnp.exp(-rate[reg(place, m), :])

    rates[0].wait()
    turn(db, rate, 0)
    decays(0)
    for n, m in enumerate(modes):
        fade8[reg(0, n), :] = jnp.exp(-float(BLOCK) * rate[reg(0, m), :])

    def arrive(place, c):
        load(k_hbm, kb, k_sem, place, c).wait()
        load(v_hbm, vb, v_sem, place, c).wait()

    def spread(place, t, to):
        for b in range(SUBS):
            lanes = pl.ds(b * LANES, LANES)
            for i in range(0, STEP, TILE):
                at = pl.ds(t + i, TILE)
                x = kb[place, at, lanes].astype(F32) * vb[place, at, lanes].astype(F32)
                for j in range(0, TILE, SUBS):
                    xb[tile(place, to + i + j, b), :] = x[j : j + SUBS]

    def read(place, t):
        return [xb[row(place, t + j), :] for j in range(BLOCK)]

    def gather(slots, look, first, size, held):
        def body(i, held):
            t = pl.multiple_of(first + i * STEP, STEP)
            held = list(held)
            for s in range(0, STEP, BLOCK):
                xs = read(0, t + s)
                for at, n in enumerate(slots):
                    a = fade[reg(0, n), :]
                    e = xs[0]
                    for x in xs[1:]:
                        e = e * a + x
                    left[(t + s) // BLOCK, n] = e
                    held[at] = held[at] * fade8[reg(0, n), :] + e
            if look:
                spread(0, pl.multiple_of(jnp.minimum(t + STEP, first + size - STEP), STEP), t + STEP)
            return tuple(held)

        return lax.fori_loop(0, size // STEP, body, held)

    zeros = jnp.zeros((SUBS, LANES), F32)

    def leave(slots, held):
        for at, n in enumerate(slots):
            ends[n] = held[at]

    slots = range(2 * OWNED)
    held = (zeros,) * len(slots)
    for c in range(CHUNKS):
        arrive(0, c)
        spread(0, c * chunk, c * chunk)
        held = gather(slots, True, c * chunk, chunk, held)
    leave(slots, held)
    pl.semaphore_wait(barrier, 3 * SIDE - 2)
    to_owner(0).start()
    to_owner(1).start()
    for k in range(2, SIDE):
        slots = range(k * OWNED, (k + 1) * OWNED)
        leave(slots, gather(slots, False, 0, ROWS, (zeros,) * OWNED))
        if k != SELF:
            to_owner(k).start()
    for e in range(OWNED):
        heard[y, e] = ends[SELF * OWNED + e]

    rates[1].wait()
    turn(db, rate, 1)
    decays(1)
    for copy in others:
        copy.wait()
    for place in range(2):
        turn(rb, raw, place)
        for n, m in enumerate(modes):
            amp[reg(place, n), :] = raw[reg(place, m), :] * jnp.sqrt(rate[reg(place, m), :])
    terms = [amp[reg(0, n), :] for n in range(MODES)]
    for j in range(BLOCK):
        total = sum(terms[1:], terms[0])
        taps[reg(0, j), :] = total + gb[0] if j == 0 else total
        if j < BLOCK - 1:
            terms = [term * fade[reg(0, n), :] for n, term in enumerate(terms)]
        if j == 0:
            for n, term in enumerate(terms):
                lead[reg(0, n), :] = term

    def own(i, carry):
        t = pl.multiple_of(i * STEP, STEP)
        for s in range(0, STEP, BLOCK):
            xs = read(0, t + s)
            for j in range(BLOCK):
                out = taps[reg(0, 0), :] * xs[j]
                for i in range(j):
                    out = out + taps[reg(0, j - i), :] * xs[i]
                xb[row(0, t + s + j), :] = out
        return carry

    def other(i, held):
        t = pl.multiple_of(i * STEP, STEP)
        held = list(held)
        g = gb[1]
        for s in range(0, STEP, BLOCK):
            xs = read(1, t + s)
            ys = [g * x for x in xs]
            for n in range(MODES):
                a = fade[reg(1, n), :]
                w = amp[reg(1, n), :]
                for j in range(BLOCK):
                    held[n] = held[n] * a + xs[j]
                    ys[j] = ys[j] + w * held[n]
            for j in range(BLOCK):
                xb[row(1, t + s + j), :] = ys[j]
        spread(1, pl.multiple_of(jnp.minimum(t + STEP, ROWS - STEP), STEP), t + STEP)
        return tuple(held)

    steps = ROWS // STEP

    def by_place(*choices):
        return jnp.where(y < 2, jnp.where(y == 0, choices[0], choices[1]), jnp.where(y == 2, choices[2], choices[3]))

    part_a = by_place(7, 4, 0, 1)
    part_b = jnp.where(z == 0, part_a, jnp.where(z == SIDE - 1, by_place(16, 13, 9, 10), by_place(11, 8, 4, 6)))

    lax.fori_loop(0, steps, own, 0)
    for c in range(CHUNKS):
        arrive(1, c)
    spread(1, 0, 0)
    held = lax.fori_loop(0, part_a, other, (zeros,) * MODES)

    for k in range(SIDE):
        if k != SELF:
            to_owner(k).wait()
    for e in range(OWNED):
        whole = jnp.exp(-float(ROWS) * rate[reg(0, y * OWNED + e), :])
        total = zeros
        for place in range(SIDE):
            before[place, e] = total
            total = total * whole + heard[place, e]
        sums[e] = total
    for dz in range(1, SIDE):

        @pl.when(z + dz < SIDE)
        def _(dz=dz):
            to_later(dz).start()

    held = lax.fori_loop(part_a, part_b, other, held)

    for dz in range(1, SIDE):

        @pl.when(z - dz >= 0)
        def _(dz=dz):
            to_later(dz).wait_recv()

    for e in range(OWNED):
        d = rate[reg(0, y * OWNED + e), :]
        row_long = jnp.exp(-float(SIDE * ROWS) * d)
        whole = jnp.exp(-float(ROWS) * d)
        total = lax.fori_loop(0, z, lambda i, total: total * row_long + earlier[i, e], zeros)
        for place in range(SIDE):
            starts[place, e] = total + before[place, e]
            total = total * whole
    for k in range(SIDE):
        if k != SELF:
            to_same(k).start()
        to_twin(k).start()
    for e in range(OWNED):
        enter[0, SELF * OWNED + e] = starts[y, e]

    lax.fori_loop(part_b, steps, other, held)

    for dz in range(1, SIDE):

        @pl.when(z + dz < SIDE)
        def _(dz=dz):
            to_later(dz).wait_send()

    def pour(blocks):
        slots = [k * OWNED + e for k in blocks for e in range(OWNED)]

        def body(i, state):
            t = pl.multiple_of(i * STEP, STEP)
            state = list(state)
            for s in range(0, STEP, BLOCK):
                ys = read(0, t + s)
                for at, n in enumerate(slots):
                    a = fade[reg(0, n), :]
                    now = state[at] * lead[reg(0, n), :]
                    ys[0] = ys[0] + now
                    for j in range(1, BLOCK):
                        now = now * a
                        ys[j] = ys[j] + now
                    state[at] = state[at] * fade8[reg(0, n), :] + left[(t + s) // BLOCK, n]
                for j in range(BLOCK):
                    xb[row(0, t + s + j), :] = ys[j]
            return tuple(state)

        lax.fori_loop(0, steps, body, tuple(enter[0, n] for n in slots))

    pour((SELF,))
    to_same(BACK[1]).wait()
    to_same(BACK[2]).wait()
    pour((1, 2))
    to_same(BACK[0]).wait()
    pour((0,))
    for p in range(2):
        for c in range(CHUNKS):
            load(q_hbm, qb, q_sem, p, c).wait()
    for k in range(SIDE):
        to_twin(k).wait()


def second_kernel(xs, enter, fade, amp, qb, o_hbm, xb, state, ob, o_sem):
    group = SUBS * LANES
    chunk = ROWS // CHUNKS
    half = lax.axis_index("half")
    owner = (half, 1 - half)

    def store(place, c):
        at = pl.ds(c * chunk, chunk)
        columns = pl.ds(pl.multiple_of(owner[place] * group, group), group)
        return pltpu.make_async_copy(ob.at[place, at, :], o_hbm.at[at, columns], o_sem.at[place, c])

    def gate(place, t, turned):
        for b in range(SUBS):
            lanes = pl.ds(b * LANES, LANES)
            out = jnp.concatenate([turned(j, b) for j in range(0, TILE, SUBS)])
            ob[place, pl.ds(t, TILE), lanes] = (qb[place, pl.ds(t, TILE), lanes].astype(F32) * out).astype(jnp.bfloat16)

    for c in range(CHUNKS):

        def plain(i, carry, first=c * chunk):
            t = pl.multiple_of(first + i * TILE, TILE)
            gate(0, t, lambda j, b: xs[tile(0, t + j, b), :])
            return carry

        lax.fori_loop(0, chunk // TILE, plain, 0)
        store(0, c).start()
    for n in range(MODES):
        state[n] = amp[reg(1, n), :] * enter[1, n]
    for c in range(CHUNKS):

        def body(i, carry, first=c * chunk):
            t = pl.multiple_of(first + i * TILE, TILE)
            for s in range(0, TILE, BLOCK):
                ys = [xs[row(1, t + s + j), :] for j in range(BLOCK)]
                for n in range(MODES):
                    a = fade[reg(1, n), :]
                    now = state[n]
                    for j in range(BLOCK):
                        now = now * a
                        ys[j] = ys[j] + now
                    state[n] = now
                for j in range(BLOCK):
                    xb[pl.ds((s + j) * SUBS, SUBS), :] = ys[j]
            gate(1, t, lambda j, b: xb[pl.ds(j * SUBS + b, SUBS, stride=SUBS), :])
            return carry

        lax.fori_loop(0, chunk // TILE, body, 0)
        store(1, c).start()
    for place in range(2):
        for c in range(CHUNKS):
            store(place, c).wait()


def shards(query_gate, key_gate, value_input, residues, decays, skip_gain):
    rows, width = key_gate.shape
    group = width // 2
    assert group == SUBS * LANES and rows == ROWS
    assert residues.shape[0] == MODES and lax.axis_size("ctx") == SIDE * SIDE
    wide = pltpu.VMEM((2, rows, group), jnp.bfloat16)
    table = (2 * MODES * SUBS, LANES)
    dma = pltpu.SemaphoreType.DMA
    hbm = pl.BlockSpec(memory_space=pltpu.HBM)
    vmem = pl.BlockSpec(memory_space=pltpu.VMEM)

    def registers(*shape):
        return pltpu.VMEM((*shape, SUBS, LANES), F32)

    operands = (query_gate, key_gate, value_input, residues, decays, skip_gain.reshape(2 * SUBS, LANES))
    kept = pl.pallas_call(
        first_kernel,
        out_shape=[
            jax.ShapeDtypeStruct((2 * SPAN * SUBS, LANES), F32),
            jax.ShapeDtypeStruct((2, MODES, SUBS, LANES), F32),
            jax.ShapeDtypeStruct(table, F32),
            jax.ShapeDtypeStruct(table, F32),
            jax.ShapeDtypeStruct((2, rows, group), jnp.bfloat16),
        ],
        in_specs=[hbm] * 6,
        out_specs=[vmem] * 5,
        scratch_shapes=[wide, wide]
        + [pltpu.VMEM((2, MODES, group), F32)] * 2
        + [registers(2)]
        + [pltpu.VMEM(table, F32)] * 5
        + [
            registers(rows // BLOCK, MODES),
            registers(MODES),
            registers(SIDE, OWNED),
            registers(OWNED),
            registers(SIDE, OWNED),
            registers(SIDE, OWNED),
            registers(SIDE, OWNED),
            dma((2, 3)),
        ]
        + [dma((2, CHUNKS))] * 3
        + [dma((SIDE,))] * 8,
        compiler_params=pltpu.CompilerParams(
            collective_id=0, has_side_effects=True, vmem_limit_bytes=FIRST_VMEM
        ),
    )(*(pltpu.with_memory_space_constraint(x, pltpu.HBM) for x in operands))
    return pl.pallas_call(
        second_kernel,
        out_shape=jax.ShapeDtypeStruct((rows, width), jnp.bfloat16),
        in_specs=[vmem] * 5,
        out_specs=hbm,
        scratch_shapes=[pltpu.VMEM((TILE * SUBS, LANES), F32), registers(MODES), wide, dma((2, CHUNKS))],
        compiler_params=pltpu.CompilerParams(vmem_limit_bytes=SECOND_VMEM),
    )(*kept)


def solution(mesh):
    placed = (
        P("ctx", "chan"),
        P("ctx", "chan"),
        P("ctx", "chan"),
        P(None, "chan"),
        P(None, "chan"),
        P("chan"),
    )
    return jax.shard_map(shards, mesh=mesh, in_specs=placed, out_specs=P("ctx", "chan"), check_vma=False)
```

```python
import jax
import jax.numpy as jnp
from jax import lax
from jax.experimental import pallas as pl
from jax.experimental.pallas import tpu as pltpu
from jax.sharding import PartitionSpec as P

F32 = jnp.float32
LANES = 128
SUBS = 8
TILE = 16
BLOCK = 8
STEP = 32
ROWS = 512
SPAN = ROWS + STEP
CHUNKS = 4
SIDE = 4
MODES = 16
OWNED = MODES // SIDE
AWAY = (2, 1, 3, 0)
BACK = tuple(AWAY.index(-a % SIDE) for a in AWAY)
SELF = SIDE - 1
FIRST_VMEM = 36 << 20
SECOND_VMEM = 36 << 20


def reg(place, n):
    return pl.ds(pl.multiple_of((place * MODES + n) * SUBS, SUBS), SUBS)


def row(place, t):
    return pl.ds(pl.multiple_of((place * SPAN + t) * SUBS, SUBS), SUBS)


def tile(place, t, b):
    return pl.ds((place * SPAN + t) * SUBS + b, SUBS, stride=SUBS)


def first_kernel(
    q_hbm, k_hbm, v_hbm, r_hbm, d_hbm, g_hbm, xb, enter, fade, amp, qb,
    kb, vb, rb, db, gb, rate, raw, fade8, lead, taps, left, ends, heard, sums, earlier, before, starts,
    p_sem, k_sem, v_sem, q_sem, a_send, a_recv, b_send, b_recv, c_send, c_recv, t_send, t_recv,
):
    group = SUBS * LANES
    chunk = ROWS // CHUNKS
    half = lax.axis_index("half")
    ctx = lax.axis_index("ctx")
    z = ctx // SIDE
    y = lax.rem(ctx, SIDE)
    owner = (half, 1 - half)

    def columns(place):
        return pl.ds(pl.multiple_of(owner[place] * group, group), group)

    def load(hbm, buf, sem, place, c):
        at = pl.ds(c * chunk, chunk)
        return pltpu.make_async_copy(hbm.at[at, columns(place)], buf.at[place, at, :], sem.at[place, c])

    def remote(src, dst, send_sem, recv_sem, to_half, to_z, to_y):
        return pltpu.make_async_remote_copy(
            src_ref=src,
            dst_ref=dst,
            send_sem=send_sem,
            recv_sem=recv_sem,
            device_id={"half": to_half, "ctx": to_z * SIDE + to_y},
            device_id_type=pl.DeviceIdType.MESH,
        )

    def along(k):
        return lax.rem(y + AWAY[k], SIDE)

    def to_owner(k):
        return remote(
            ends.at[pl.ds(k * OWNED, OWNED)], heard.at[y], a_send.at[k], a_recv.at[k], half, z, along(k)
        )

    def to_later(dz):
        return remote(sums, earlier.at[z], b_send.at[dz - 1], b_recv.at[dz - 1], half, lax.rem(z + dz, SIDE), y)

    def to_same(k):
        return remote(
            starts.at[along(k)], enter.at[0, pl.ds(BACK[k] * OWNED, OWNED)], c_send.at[k], c_recv.at[k], half, z, along(k)
        )

    def to_twin(k):
        return remote(
            starts.at[along(k)], enter.at[1, pl.ds(BACK[k] * OWNED, OWNED)], t_send.at[k], t_recv.at[k], 1 - half, z, along(k)
        )

    barrier = pltpu.get_barrier_semaphore()

    def greet(to_half, to_z, to_y):
        pl.semaphore_signal(
            barrier,
            inc=1,
            device_id={"half": to_half, "ctx": to_z * SIDE + to_y},
            device_id_type=pl.DeviceIdType.MESH,
        )

    rates = [pltpu.make_async_copy(d_hbm.at[:, columns(p)], db.at[p], p_sem.at[p, 0]) for p in range(2)]
    others = [pltpu.make_async_copy(r_hbm.at[:, columns(p)], rb.at[p], p_sem.at[p, 1]) for p in range(2)]
    others += [
        pltpu.make_async_copy(
            g_hbm.at[pl.ds(pl.multiple_of(owner[p] * SUBS, SUBS), SUBS), :], gb.at[p], p_sem.at[p, 2]
        )
        for p in range(2)
    ]
    rates[0].start()
    for c in range(CHUNKS):
        load(k_hbm, kb, k_sem, 0, c).start()
        load(v_hbm, vb, v_sem, 0, c).start()
    for k in range(SIDE):
        if k != SELF:
            greet(half, z, along(k))
        greet(1 - half, z, along(k))
    for dz in range(1, SIDE):
        greet(half, lax.rem(z + dz, SIDE), y)
    rates[1].start()
    for copy in others:
        copy.start()
    for c in range(CHUNKS):
        load(k_hbm, kb, k_sem, 1, c).start()
        load(v_hbm, vb, v_sem, 1, c).start()
    for p in range(2):
        for c in range(CHUNKS):
            load(q_hbm, qb, q_sem, p, c).start()

    def turn(src, dst, place):
        for b in range(SUBS):
            lanes = pl.ds(b * LANES, LANES)
            for m in range(0, MODES, SUBS):
                at = pl.ds((place * MODES + m) * SUBS + b, SUBS, stride=SUBS)
                dst[at, :] = src[place, m : m + SUBS, lanes]

    modes = [along(k) * OWNED + e for k in range(SIDE) for e in range(OWNED)]

    def decays(place):
        for n, m in enumerate(modes):
            fade[reg(place, n), :] = jnp.exp(-rate[reg(place, m), :])

    rates[0].wait()
    turn(db, rate, 0)
    decays(0)
    for n, m in enumerate(modes):
        fade8[reg(0, n), :] = jnp.exp(-float(BLOCK) * rate[reg(0, m), :])

    def arrive(place, c):
        load(k_hbm, kb, k_sem, place, c).wait()
        load(v_hbm, vb, v_sem, place, c).wait()

    def spread(place, t, to):
        for b in range(SUBS):
            lanes = pl.ds(b * LANES, LANES)
            for i in range(0, STEP, TILE):
                at = pl.ds(t + i, TILE)
                x = kb[place, at, lanes].astype(F32) * vb[place, at, lanes].astype(F32)
                for j in range(0, TILE, SUBS):
                    xb[tile(place, to + i + j, b), :] = x[j : j + SUBS]

    def read(place, t):
        return [xb[row(place, t + j), :] for j in range(BLOCK)]

    def gather(slots, look, first, size, held):
        def body(i, held):
            t = pl.multiple_of(first + i * STEP, STEP)
            held = list(held)
            for s in range(0, STEP, BLOCK):
                xs = read(0, t + s)
                for at, n in enumerate(slots):
                    a = fade[reg(0, n), :]
                    e = xs[0]
                    for x in xs[1:]:
                        e = e * a + x
                    left[(t + s) // BLOCK, n] = e
                    held[at] = held[at] * fade8[reg(0, n), :] + e
            if look:
                spread(0, pl.multiple_of(jnp.minimum(t + STEP, first + size - STEP), STEP), t + STEP)
            return tuple(held)

        return lax.fori_loop(0, size // STEP, body, held)

    zeros = jnp.zeros((SUBS, LANES), F32)

    def leave(slots, held):
        for at, n in enumerate(slots):
            ends[n] = held[at]

    slots = range(2 * OWNED)
    held = (zeros,) * len(slots)
    for c in range(CHUNKS):
        arrive(0, c)
        spread(0, c * chunk, c * chunk)
        held = gather(slots, True, c * chunk, chunk, held)
    leave(slots, held)
    pl.semaphore_wait(barrier, 3 * SIDE - 2)
    to_owner(0).start()
    to_owner(1).start()
    for k in range(2, SIDE):
        slots = range(k * OWNED, (k + 1) * OWNED)
        leave(slots, gather(slots, False, 0, ROWS, (zeros,) * OWNED))
        if k != SELF:
            to_owner(k).start()
    for e in range(OWNED):
        heard[y, e] = ends[SELF * OWNED + e]

    rates[1].wait()
    turn(db, rate, 1)
    decays(1)
    for copy in others:
        copy.wait()
    for place in range(2):
        turn(rb, raw, place)
        for n, m in enumerate(modes):
            amp[reg(place, n), :] = raw[reg(place, m), :] * jnp.sqrt(rate[reg(place, m), :])
    terms = [amp[reg(0, n), :] for n in range(MODES)]
    for j in range(BLOCK):
        total = sum(terms[1:], terms[0])
        taps[reg(0, j), :] = total + gb[0] if j == 0 else total
        if j < BLOCK - 1:
            terms = [term * fade[reg(0, n), :] for n, term in enumerate(terms)]
        if j == 0:
            for n, term in enumerate(terms):
                lead[reg(0, n), :] = term

    def own(i, carry):
        t = pl.multiple_of(i * STEP, STEP)
        for s in range(0, STEP, BLOCK):
            xs = read(0, t + s)
            for j in range(BLOCK):
                out = taps[reg(0, 0), :] * xs[j]
                for i in range(j):
                    out = out + taps[reg(0, j - i), :] * xs[i]
                xb[row(0, t + s + j), :] = out
        return carry

    def other(i, held):
        t = pl.multiple_of(i * STEP, STEP)
        held = list(held)
        g = gb[1]
        for s in range(0, STEP, BLOCK):
            xs = read(1, t + s)
            ys = [g * x for x in xs]
            for n in range(MODES):
                a = fade[reg(1, n), :]
                w = amp[reg(1, n), :]
                for j in range(BLOCK):
                    held[n] = held[n] * a + xs[j]
                    ys[j] = ys[j] + w * held[n]
            for j in range(BLOCK):
                xb[row(1, t + s + j), :] = ys[j]
        spread(1, pl.multiple_of(jnp.minimum(t + STEP, ROWS - STEP), STEP), t + STEP)
        return tuple(held)

    steps = ROWS // STEP

    def by_place(*choices):
        return jnp.where(y < 2, jnp.where(y == 0, choices[0], choices[1]), jnp.where(y == 2, choices[2], choices[3]))

    part_a = by_place(7, 4, 4, 2)
    part_b = jnp.where(z == 0, part_a, jnp.where(z == SIDE - 1, by_place(16, 12, 12, 11), by_place(11, 8, 9, 7)))

    lax.fori_loop(0, steps, own, 0)
    for c in range(CHUNKS):
        arrive(1, c)
    spread(1, 0, 0)
    held = lax.fori_loop(0, part_a, other, (zeros,) * MODES)

    for k in range(SIDE):
        if k != SELF:
            to_owner(k).wait()
    for e in range(OWNED):
        whole = jnp.exp(-float(ROWS) * rate[reg(0, y * OWNED + e), :])
        total = zeros
        for place in range(SIDE):
            before[place, e] = total
            total = total * whole + heard[place, e]
        sums[e] = total
    for dz in range(1, SIDE):

        @pl.when(z + dz < SIDE)
        def _(dz=dz):
            to_later(dz).start()

    held = lax.fori_loop(part_a, part_b, other, held)

    for dz in range(1, SIDE):

        @pl.when(z - dz >= 0)
        def _(dz=dz):
            to_later(dz).wait_recv()

    for e in range(OWNED):
        d = rate[reg(0, y * OWNED + e), :]
        row_long = jnp.exp(-float(SIDE * ROWS) * d)
        whole = jnp.exp(-float(ROWS) * d)
        total = lax.fori_loop(0, z, lambda i, total: total * row_long + earlier[i, e], zeros)
        for place in range(SIDE):
            starts[place, e] = total + before[place, e]
            total = total * whole
    for k in range(SIDE):
        if k != SELF:
            to_same(k).start()
        to_twin(k).start()
    for e in range(OWNED):
        enter[0, SELF * OWNED + e] = starts[y, e]

    lax.fori_loop(part_b, steps, other, held)

    for dz in range(1, SIDE):

        @pl.when(z + dz < SIDE)
        def _(dz=dz):
            to_later(dz).wait_send()

    def pour(blocks):
        slots = [k * OWNED + e for k in blocks for e in range(OWNED)]

        def body(i, state):
            t = pl.multiple_of(i * STEP, STEP)
            state = list(state)
            for s in range(0, STEP, BLOCK):
                ys = read(0, t + s)
                for at, n in enumerate(slots):
                    a = fade[reg(0, n), :]
                    now = state[at] * lead[reg(0, n), :]
                    ys[0] = ys[0] + now
                    for j in range(1, BLOCK):
                        now = now * a
                        ys[j] = ys[j] + now
                    state[at] = state[at] * fade8[reg(0, n), :] + left[(t + s) // BLOCK, n]
                for j in range(BLOCK):
                    xb[row(0, t + s + j), :] = ys[j]
            return tuple(state)

        lax.fori_loop(0, steps, body, tuple(enter[0, n] for n in slots))

    pour((SELF,))
    to_same(BACK[1]).wait()
    to_same(BACK[2]).wait()
    pour((1, 2))
    to_same(BACK[0]).wait()
    pour((0,))
    for p in range(2):
        for c in range(CHUNKS):
            load(q_hbm, qb, q_sem, p, c).wait()
    for k in range(SIDE):
        to_twin(k).wait()


def second_kernel(xs, enter, fade, amp, qb, o_hbm, xb, state, ob, o_sem):
    group = SUBS * LANES
    chunk = ROWS // CHUNKS
    half = lax.axis_index("half")
    owner = (half, 1 - half)

    def store(place, c):
        at = pl.ds(c * chunk, chunk)
        columns = pl.ds(pl.multiple_of(owner[place] * group, group), group)
        return pltpu.make_async_copy(ob.at[place, at, :], o_hbm.at[at, columns], o_sem.at[place, c])

    def gate(place, t, turned):
        for b in range(SUBS):
            lanes = pl.ds(b * LANES, LANES)
            out = jnp.concatenate([turned(j, b) for j in range(0, TILE, SUBS)])
            ob[place, pl.ds(t, TILE), lanes] = (qb[place, pl.ds(t, TILE), lanes].astype(F32) * out).astype(jnp.bfloat16)

    for n in range(MODES):
        state[n] = amp[reg(1, n), :] * enter[1, n]
    for c in range(CHUNKS):

        def body(i, carry, first=c * chunk):
            t = pl.multiple_of(first + i * STEP, STEP)
            for s in range(0, STEP, BLOCK):
                ys = [xs[row(1, t + s + j), :] for j in range(BLOCK)]
                for n in range(MODES):
                    a = fade[reg(1, n), :]
                    now = state[n]
                    for j in range(BLOCK):
                        now = now * a
                        ys[j] = ys[j] + now
                    state[n] = now
                for j in range(BLOCK):
                    xb[pl.ds((s + j) * SUBS, SUBS), :] = ys[j]
                if (s + BLOCK) % TILE == 0:
                    at = s + BLOCK - TILE
                    gate(0, t + at, lambda j, b, at=at: xs[tile(0, t + at + j, b), :])
                    gate(1, t + at, lambda j, b, at=at: xb[pl.ds((at + j) * SUBS + b, SUBS, stride=SUBS), :])
            return carry

        lax.fori_loop(0, chunk // STEP, body, 0)
        store(0, c).start()
        store(1, c).start()
    for place in range(2):
        for c in range(CHUNKS):
            store(place, c).wait()


def shards(query_gate, key_gate, value_input, residues, decays, skip_gain):
    rows, width = key_gate.shape
    group = width // 2
    assert group == SUBS * LANES and rows == ROWS
    assert residues.shape[0] == MODES and lax.axis_size("ctx") == SIDE * SIDE
    wide = pltpu.VMEM((2, rows, group), jnp.bfloat16)
    table = (2 * MODES * SUBS, LANES)
    dma = pltpu.SemaphoreType.DMA
    hbm = pl.BlockSpec(memory_space=pltpu.HBM)
    vmem = pl.BlockSpec(memory_space=pltpu.VMEM)

    def registers(*shape):
        return pltpu.VMEM((*shape, SUBS, LANES), F32)

    operands = (query_gate, key_gate, value_input, residues, decays, skip_gain.reshape(2 * SUBS, LANES))
    kept = pl.pallas_call(
        first_kernel,
        out_shape=[
            jax.ShapeDtypeStruct((2 * SPAN * SUBS, LANES), F32),
            jax.ShapeDtypeStruct((2, MODES, SUBS, LANES), F32),
            jax.ShapeDtypeStruct(table, F32),
            jax.ShapeDtypeStruct(table, F32),
            jax.ShapeDtypeStruct((2, rows, group), jnp.bfloat16),
        ],
        in_specs=[hbm] * 6,
        out_specs=[vmem] * 5,
        scratch_shapes=[wide, wide]
        + [pltpu.VMEM((2, MODES, group), F32)] * 2
        + [registers(2)]
        + [pltpu.VMEM(table, F32)] * 5
        + [
            registers(rows // BLOCK, MODES),
            registers(MODES),
            registers(SIDE, OWNED),
            registers(OWNED),
            registers(SIDE, OWNED),
            registers(SIDE, OWNED),
            registers(SIDE, OWNED),
            dma((2, 3)),
        ]
        + [dma((2, CHUNKS))] * 3
        + [dma((SIDE,))] * 8,
        compiler_params=pltpu.CompilerParams(
            collective_id=0, has_side_effects=True, vmem_limit_bytes=FIRST_VMEM
        ),
    )(*(pltpu.with_memory_space_constraint(x, pltpu.HBM) for x in operands))
    return pl.pallas_call(
        second_kernel,
        out_shape=jax.ShapeDtypeStruct((rows, width), jnp.bfloat16),
        in_specs=[vmem] * 5,
        out_specs=hbm,
        scratch_shapes=[pltpu.VMEM((STEP * SUBS, LANES), F32), registers(MODES), wide, dma((2, CHUNKS))],
        compiler_params=pltpu.CompilerParams(vmem_limit_bytes=SECOND_VMEM),
    )(*kept)


def solution(mesh):
    placed = (
        P("ctx", "chan"),
        P("ctx", "chan"),
        P("ctx", "chan"),
        P(None, "chan"),
        P(None, "chan"),
        P("chan"),
    )
    return jax.shard_map(shards, mesh=mesh, in_specs=placed, out_specs=P("ctx", "chan"), check_vma=False)
```

```python
import jax
import jax.numpy as jnp
from jax import lax
from jax.experimental import pallas as pl
from jax.experimental.pallas import tpu as pltpu
from jax.sharding import PartitionSpec as P

F32 = jnp.float32
LANES = 128
SUBS = 8
TILE = 16
BLOCK = 8
STEP = 32
ROWS = 512
SPAN = ROWS + STEP
CHUNKS = 4
SIDE = 4
MODES = 16
OWNED = MODES // SIDE
AWAY = (2, 1, 3, 0)
BACK = tuple(AWAY.index(-a % SIDE) for a in AWAY)
SELF = SIDE - 1
FIRST_VMEM = 36 << 20
SECOND_VMEM = 36 << 20


def reg(place, n):
    return pl.ds(pl.multiple_of((place * MODES + n) * SUBS, SUBS), SUBS)


def row(place, t):
    return pl.ds(pl.multiple_of((place * SPAN + t) * SUBS, SUBS), SUBS)


def tile(place, t, b):
    return pl.ds((place * SPAN + t) * SUBS + b, SUBS, stride=SUBS)


def first_kernel(
    q_hbm, k_hbm, v_hbm, r_hbm, d_hbm, g_hbm, xb, enter, fade, amp, qb,
    kb, vb, rb, db, gb, rate, raw, fade8, lead, taps, left, ends, heard, sums, earlier, before, starts,
    p_sem, k_sem, v_sem, q_sem, a_send, a_recv, b_send, b_recv, c_send, c_recv, t_send, t_recv,
):
    group = SUBS * LANES
    chunk = ROWS // CHUNKS
    half = lax.axis_index("half")
    ctx = lax.axis_index("ctx")
    z = ctx // SIDE
    y = lax.rem(ctx, SIDE)
    owner = (half, 1 - half)

    def columns(place):
        return pl.ds(pl.multiple_of(owner[place] * group, group), group)

    def load(hbm, buf, sem, place, c):
        at = pl.ds(c * chunk, chunk)
        return pltpu.make_async_copy(hbm.at[at, columns(place)], buf.at[place, at, :], sem.at[place, c])

    def remote(src, dst, send_sem, recv_sem, to_half, to_z, to_y):
        return pltpu.make_async_remote_copy(
            src_ref=src,
            dst_ref=dst,
            send_sem=send_sem,
            recv_sem=recv_sem,
            device_id={"half": to_half, "ctx": to_z * SIDE + to_y},
            device_id_type=pl.DeviceIdType.MESH,
        )

    def along(k):
        return lax.rem(y + AWAY[k], SIDE)

    def to_owner(k):
        return remote(
            ends.at[pl.ds(k * OWNED, OWNED)], heard.at[y], a_send.at[k], a_recv.at[k], half, z, along(k)
        )

    def to_later(dz):
        return remote(sums, earlier.at[z], b_send.at[dz - 1], b_recv.at[dz - 1], half, lax.rem(z + dz, SIDE), y)

    def to_same(k):
        return remote(
            starts.at[along(k)], enter.at[0, pl.ds(BACK[k] * OWNED, OWNED)], c_send.at[k], c_recv.at[k], half, z, along(k)
        )

    def to_twin(k):
        return remote(
            starts.at[along(k)], enter.at[1, pl.ds(BACK[k] * OWNED, OWNED)], t_send.at[k], t_recv.at[k], 1 - half, z, along(k)
        )

    barrier = pltpu.get_barrier_semaphore()

    def greet(to_half, to_z, to_y):
        pl.semaphore_signal(
            barrier,
            inc=1,
            device_id={"half": to_half, "ctx": to_z * SIDE + to_y},
            device_id_type=pl.DeviceIdType.MESH,
        )

    rates = [pltpu.make_async_copy(d_hbm.at[:, columns(p)], db.at[p], p_sem.at[p, 0]) for p in range(2)]
    others = [pltpu.make_async_copy(r_hbm.at[:, columns(p)], rb.at[p], p_sem.at[p, 1]) for p in range(2)]
    others += [
        pltpu.make_async_copy(
            g_hbm.at[pl.ds(pl.multiple_of(owner[p] * SUBS, SUBS), SUBS), :], gb.at[p], p_sem.at[p, 2]
        )
        for p in range(2)
    ]
    rates[0].start()
    for c in range(CHUNKS):
        load(k_hbm, kb, k_sem, 0, c).start()
        load(v_hbm, vb, v_sem, 0, c).start()
    for k in range(SIDE):
        if k != SELF:
            greet(half, z, along(k))
        greet(1 - half, z, along(k))
    for dz in range(1, SIDE):
        greet(half, lax.rem(z + dz, SIDE), y)
    rates[1].start()
    for copy in others:
        copy.start()
    for c in range(CHUNKS):
        load(k_hbm, kb, k_sem, 1, c).start()
        load(v_hbm, vb, v_sem, 1, c).start()
    for p in range(2):
        for c in range(CHUNKS):
            load(q_hbm, qb, q_sem, p, c).start()

    def turn(src, dst, place):
        for b in range(SUBS):
            lanes = pl.ds(b * LANES, LANES)
            for m in range(0, MODES, SUBS):
                at = pl.ds((place * MODES + m) * SUBS + b, SUBS, stride=SUBS)
                dst[at, :] = src[place, m : m + SUBS, lanes]

    modes = [along(k) * OWNED + e for k in range(SIDE) for e in range(OWNED)]

    def decays(place):
        for n, m in enumerate(modes):
            fade[reg(place, n), :] = jnp.exp(-rate[reg(place, m), :])

    rates[0].wait()
    turn(db, rate, 0)
    decays(0)
    for n, m in enumerate(modes):
        fade8[reg(0, n), :] = jnp.exp(-float(BLOCK) * rate[reg(0, m), :])

    def arrive(place, c):
        load(k_hbm, kb, k_sem, place, c).wait()
        load(v_hbm, vb, v_sem, place, c).wait()

    def spread(place, t, to):
        for b in range(SUBS):
            lanes = pl.ds(b * LANES, LANES)
            for i in range(0, STEP, TILE):
                at = pl.ds(t + i, TILE)
                x = kb[place, at, lanes].astype(F32) * vb[place, at, lanes].astype(F32)
                for j in range(0, TILE, SUBS):
                    xb[tile(place, to + i + j, b), :] = x[j : j + SUBS]

    def read(place, t):
        return [xb[row(place, t + j), :] for j in range(BLOCK)]

    def gather(slots, look, first, size, held):
        def body(i, held):
            t = pl.multiple_of(first + i * STEP, STEP)
            held = list(held)
            for s in range(0, STEP, BLOCK):
                xs = read(0, t + s)
                for at, n in enumerate(slots):
                    a = fade[reg(0, n), :]
                    e = xs[0]
                    for x in xs[1:]:
                        e = e * a + x
                    left[(t + s) // BLOCK, n] = e
                    held[at] = held[at] * fade8[reg(0, n), :] + e
            if look:
                spread(0, pl.multiple_of(jnp.minimum(t + STEP, first + size - STEP), STEP), t + STEP)
            return tuple(held)

        return lax.fori_loop(0, size // STEP, body, held)

    zeros = jnp.zeros((SUBS, LANES), F32)

    def leave(slots, held):
        for at, n in enumerate(slots):
            ends[n] = held[at]

    slots = range(2 * OWNED)
    held = (zeros,) * len(slots)
    for c in range(CHUNKS):
        arrive(0, c)
        spread(0, c * chunk, c * chunk)
        held = gather(slots, True, c * chunk, chunk, held)
    leave(slots, held)
    pl.semaphore_wait(barrier, 3 * SIDE - 2)
    to_owner(0).start()
    to_owner(1).start()
    for k in range(2, SIDE):
        slots = range(k * OWNED, (k + 1) * OWNED)
        leave(slots, gather(slots, False, 0, ROWS, (zeros,) * OWNED))
        if k != SELF:
            to_owner(k).start()
    for e in range(OWNED):
        heard[y, e] = ends[SELF * OWNED + e]

    rates[1].wait()
    turn(db, rate, 1)
    decays(1)
    for copy in others:
        copy.wait()
    for place in range(2):
        turn(rb, raw, place)
        for n, m in enumerate(modes):
            amp[reg(place, n), :] = raw[reg(place, m), :] * jnp.sqrt(rate[reg(place, m), :])
    terms = [amp[reg(0, n), :] for n in range(MODES)]
    for j in range(BLOCK):
        total = sum(terms[1:], terms[0])
        taps[reg(0, j), :] = total + gb[0] if j == 0 else total
        if j < BLOCK - 1:
            terms = [term * fade[reg(0, n), :] for n, term in enumerate(terms)]
        if j == 0:
            for n, term in enumerate(terms):
                lead[reg(0, n), :] = term

    def own(i, carry):
        t = pl.multiple_of(i * STEP, STEP)
        for s in range(0, STEP, BLOCK):
            xs = read(0, t + s)
            for j in range(BLOCK):
                out = taps[reg(0, 0), :] * xs[j]
                for i in range(j):
                    out = out + taps[reg(0, j - i), :] * xs[i]
                xb[row(0, t + s + j), :] = out
        return carry

    def other(i, held):
        t = pl.multiple_of(i * STEP, STEP)
        held = list(held)
        g = gb[1]
        for s in range(0, STEP, BLOCK):
            xs = read(1, t + s)
            ys = [g * x for x in xs]
            for n in range(MODES):
                a = fade[reg(1, n), :]
                w = amp[reg(1, n), :]
                for j in range(BLOCK):
                    held[n] = held[n] * a + xs[j]
                    ys[j] = ys[j] + w * held[n]
            for j in range(BLOCK):
                xb[row(1, t + s + j), :] = ys[j]
        spread(1, pl.multiple_of(jnp.minimum(t + STEP, ROWS - STEP), STEP), t + STEP)
        return tuple(held)

    steps = ROWS // STEP

    def by_place(*choices):
        return jnp.where(y < 2, jnp.where(y == 0, choices[0], choices[1]), jnp.where(y == 2, choices[2], choices[3]))

    part_a = by_place(7, 4, 4, 2)
    part_b = jnp.where(z == 0, part_a, jnp.where(z == SIDE - 1, by_place(13, 10, 9, 8), by_place(11, 8, 9, 7)))

    lax.fori_loop(0, steps, own, 0)
    for c in range(CHUNKS):
        arrive(1, c)
    spread(1, 0, 0)
    held = lax.fori_loop(0, part_a, other, (zeros,) * MODES)

    for k in range(SIDE):
        if k != SELF:
            to_owner(k).wait()
    for e in range(OWNED):
        whole = jnp.exp(-float(ROWS) * rate[reg(0, y * OWNED + e), :])
        total = zeros
        for place in range(SIDE):
            before[place, e] = total
            total = total * whole + heard[place, e]
        sums[e] = total
    for dz in range(1, SIDE):

        @pl.when(z + dz < SIDE)
        def _(dz=dz):
            to_later(dz).start()

    held = lax.fori_loop(part_a, part_b, other, held)

    for dz in range(1, SIDE):

        @pl.when(z - dz >= 0)
        def _(dz=dz):
            to_later(dz).wait_recv()

    for e in range(OWNED):
        d = rate[reg(0, y * OWNED + e), :]
        row_long = jnp.exp(-float(SIDE * ROWS) * d)
        whole = jnp.exp(-float(ROWS) * d)
        total = lax.fori_loop(0, z, lambda i, total: total * row_long + earlier[i, e], zeros)
        for place in range(SIDE):
            starts[place, e] = total + before[place, e]
            total = total * whole
    for k in range(SIDE):
        if k != SELF:
            to_same(k).start()
        to_twin(k).start()
    for e in range(OWNED):
        enter[0, SELF * OWNED + e] = starts[y, e]

    lax.fori_loop(part_b, steps, other, held)

    for dz in range(1, SIDE):

        @pl.when(z + dz < SIDE)
        def _(dz=dz):
            to_later(dz).wait_send()

    def pour(blocks):
        slots = [k * OWNED + e for k in blocks for e in range(OWNED)]

        def body(i, state):
            t = pl.multiple_of(i * STEP, STEP)
            state = list(state)
            for s in range(0, STEP, BLOCK):
                ys = read(0, t + s)
                for at, n in enumerate(slots):
                    a = fade[reg(0, n), :]
                    now = state[at] * lead[reg(0, n), :]
                    ys[0] = ys[0] + now
                    for j in range(1, BLOCK):
                        now = now * a
                        ys[j] = ys[j] + now
                    state[at] = state[at] * fade8[reg(0, n), :] + left[(t + s) // BLOCK, n]
                for j in range(BLOCK):
                    xb[row(0, t + s + j), :] = ys[j]
            return tuple(state)

        lax.fori_loop(0, steps, body, tuple(enter[0, n] for n in slots))

    pour((SELF,))
    for k in (2, 1, 0):
        to_same(BACK[k]).wait()
        pour((k,))
    for p in range(2):
        for c in range(CHUNKS):
            load(q_hbm, qb, q_sem, p, c).wait()
    for k in range(SIDE):
        to_twin(k).wait()


def second_kernel(xs, enter, fade, amp, qb, o_hbm, xb, state, ob, o_sem):
    group = SUBS * LANES
    chunk = ROWS // CHUNKS
    half = lax.axis_index("half")
    owner = (half, 1 - half)

    def store(place, c):
        at = pl.ds(c * chunk, chunk)
        columns = pl.ds(pl.multiple_of(owner[place] * group, group), group)
        return pltpu.make_async_copy(ob.at[place, at, :], o_hbm.at[at, columns], o_sem.at[place, c])

    def gate(place, t, turned):
        for b in range(SUBS):
            lanes = pl.ds(b * LANES, LANES)
            out = jnp.concatenate([turned(j, b) for j in range(0, TILE, SUBS)])
            ob[place, pl.ds(t, TILE), lanes] = (qb[place, pl.ds(t, TILE), lanes].astype(F32) * out).astype(jnp.bfloat16)

    for n in range(MODES):
        state[n] = amp[reg(1, n), :] * enter[1, n]
    for c in range(CHUNKS):

        def body(i, carry, first=c * chunk):
            t = pl.multiple_of(first + i * STEP, STEP)
            for s in range(0, STEP, BLOCK):
                ys = [xs[row(1, t + s + j), :] for j in range(BLOCK)]
                for n in range(MODES):
                    a = fade[reg(1, n), :]
                    now = state[n]
                    for j in range(BLOCK):
                        now = now * a
                        ys[j] = ys[j] + now
                    state[n] = now
                for j in range(BLOCK):
                    xb[pl.ds((s + j) * SUBS, SUBS), :] = ys[j]
                if (s + BLOCK) % TILE == 0:
                    at = s + BLOCK - TILE
                    gate(0, t + at, lambda j, b, at=at: xs[tile(0, t + at + j, b), :])
                    gate(1, t + at, lambda j, b, at=at: xb[pl.ds((at + j) * SUBS + b, SUBS, stride=SUBS), :])
            return carry

        lax.fori_loop(0, chunk // STEP, body, 0)
        store(0, c).start()
        store(1, c).start()
    for place in range(2):
        for c in range(CHUNKS):
            store(place, c).wait()


def shards(query_gate, key_gate, value_input, residues, decays, skip_gain):
    rows, width = key_gate.shape
    group = width // 2
    assert group == SUBS * LANES and rows == ROWS
    assert residues.shape[0] == MODES and lax.axis_size("ctx") == SIDE * SIDE
    wide = pltpu.VMEM((2, rows, group), jnp.bfloat16)
    table = (2 * MODES * SUBS, LANES)
    dma = pltpu.SemaphoreType.DMA
    hbm = pl.BlockSpec(memory_space=pltpu.HBM)
    vmem = pl.BlockSpec(memory_space=pltpu.VMEM)

    def registers(*shape):
        return pltpu.VMEM((*shape, SUBS, LANES), F32)

    operands = (query_gate, key_gate, value_input, residues, decays, skip_gain.reshape(2 * SUBS, LANES))
    kept = pl.pallas_call(
        first_kernel,
        out_shape=[
            jax.ShapeDtypeStruct((2 * SPAN * SUBS, LANES), F32),
            jax.ShapeDtypeStruct((2, MODES, SUBS, LANES), F32),
            jax.ShapeDtypeStruct(table, F32),
            jax.ShapeDtypeStruct(table, F32),
            jax.ShapeDtypeStruct((2, rows, group), jnp.bfloat16),
        ],
        in_specs=[hbm] * 6,
        out_specs=[vmem] * 5,
        scratch_shapes=[wide, wide]
        + [pltpu.VMEM((2, MODES, group), F32)] * 2
        + [registers(2)]
        + [pltpu.VMEM(table, F32)] * 5
        + [
            registers(rows // BLOCK, MODES),
            registers(MODES),
            registers(SIDE, OWNED),
            registers(OWNED),
            registers(SIDE, OWNED),
            registers(SIDE, OWNED),
            registers(SIDE, OWNED),
            dma((2, 3)),
        ]
        + [dma((2, CHUNKS))] * 3
        + [dma((SIDE,))] * 8,
        compiler_params=pltpu.CompilerParams(
            collective_id=0, has_side_effects=True, vmem_limit_bytes=FIRST_VMEM
        ),
    )(*(pltpu.with_memory_space_constraint(x, pltpu.HBM) for x in operands))
    return pl.pallas_call(
        second_kernel,
        out_shape=jax.ShapeDtypeStruct((rows, width), jnp.bfloat16),
        in_specs=[vmem] * 5,
        out_specs=hbm,
        scratch_shapes=[pltpu.VMEM((STEP * SUBS, LANES), F32), registers(MODES), wide, dma((2, CHUNKS))],
        compiler_params=pltpu.CompilerParams(vmem_limit_bytes=SECOND_VMEM),
    )(*kept)


def solution(mesh):
    placed = (
        P("ctx", "chan"),
        P("ctx", "chan"),
        P("ctx", "chan"),
        P(None, "chan"),
        P(None, "chan"),
        P("chan"),
    )
    return jax.shard_map(shards, mesh=mesh, in_specs=placed, out_specs=P("ctx", "chan"), check_vma=False)
```

```python
import jax
import jax.numpy as jnp
from jax import lax
from jax.experimental import pallas as pl
from jax.experimental.pallas import tpu as pltpu
from jax.sharding import PartitionSpec as P

F32 = jnp.float32
LANES = 128
SUBS = 8
TILE = 16
BLOCK = 8
STEP = 32
WIDE = 64
ROWS = 512
SPAN = ROWS + STEP
CHUNKS = 4
PARTS = 8
SIDE = 4
MODES = 16
OWNED = MODES // SIDE
AWAY = (2, 1, 3, 0)
BACK = tuple(AWAY.index(-a % SIDE) for a in AWAY)
SELF = SIDE - 1
FIRST_VMEM = 36 << 20
SECOND_VMEM = 36 << 20


def reg(place, n):
    return pl.ds(pl.multiple_of((place * MODES + n) * SUBS, SUBS), SUBS)


def row(place, t):
    return pl.ds(pl.multiple_of((place * SPAN + t) * SUBS, SUBS), SUBS)


def tile(place, t, b):
    return pl.ds((place * SPAN + t) * SUBS + b, SUBS, stride=SUBS)


def first_kernel(
    q_hbm, k_hbm, v_hbm, r_hbm, d_hbm, g_hbm, xb, enter, fade, amp, qb,
    kb, vb, rb, db, gb, rate, raw, fade8, lead, taps, left, ends, heard, sums, earlier, before, starts,
    p_sem, k_sem, v_sem, q_sem, a_send, a_recv, b_send, b_recv, c_send, c_recv, t_send, t_recv,
):
    group = SUBS * LANES
    chunk = ROWS // CHUNKS
    half = lax.axis_index("half")
    ctx = lax.axis_index("ctx")
    z = ctx // SIDE
    y = lax.rem(ctx, SIDE)
    owner = (half, 1 - half)

    def columns(place):
        return pl.ds(pl.multiple_of(owner[place] * group, group), group)

    def load(hbm, buf, sem, place, c):
        at = pl.ds(c * chunk, chunk)
        return pltpu.make_async_copy(hbm.at[at, columns(place)], buf.at[place, at, :], sem.at[place, c])

    def remote(src, dst, send_sem, recv_sem, to_half, to_z, to_y):
        return pltpu.make_async_remote_copy(
            src_ref=src,
            dst_ref=dst,
            send_sem=send_sem,
            recv_sem=recv_sem,
            device_id={"half": to_half, "ctx": to_z * SIDE + to_y},
            device_id_type=pl.DeviceIdType.MESH,
        )

    def along(k):
        return lax.rem(y + AWAY[k], SIDE)

    def to_owner(k):
        return remote(
            ends.at[pl.ds(k * OWNED, OWNED)], heard.at[y], a_send.at[k], a_recv.at[k], half, z, along(k)
        )

    def to_later(dz):
        return remote(sums, earlier.at[z], b_send.at[dz - 1], b_recv.at[dz - 1], half, lax.rem(z + dz, SIDE), y)

    def to_same(k):
        return remote(
            starts.at[along(k)], enter.at[0, pl.ds(BACK[k] * OWNED, OWNED)], c_send.at[k], c_recv.at[k], half, z, along(k)
        )

    def to_twin(k):
        return remote(
            starts.at[along(k)], enter.at[1, pl.ds(BACK[k] * OWNED, OWNED)], t_send.at[k], t_recv.at[k], 1 - half, z, along(k)
        )

    barrier = pltpu.get_barrier_semaphore()

    def greet(to_half, to_z, to_y):
        pl.semaphore_signal(
            barrier,
            inc=1,
            device_id={"half": to_half, "ctx": to_z * SIDE + to_y},
            device_id_type=pl.DeviceIdType.MESH,
        )

    rates = [pltpu.make_async_copy(d_hbm.at[:, columns(p)], db.at[p], p_sem.at[p, 0]) for p in range(2)]
    others = [pltpu.make_async_copy(r_hbm.at[:, columns(p)], rb.at[p], p_sem.at[p, 1]) for p in range(2)]
    others += [
        pltpu.make_async_copy(
            g_hbm.at[pl.ds(pl.multiple_of(owner[p] * SUBS, SUBS), SUBS), :], gb.at[p], p_sem.at[p, 2]
        )
        for p in range(2)
    ]
    rates[0].start()
    for c in range(CHUNKS):
        load(k_hbm, kb, k_sem, 0, c).start()
        load(v_hbm, vb, v_sem, 0, c).start()
    for k in range(SIDE):
        if k != SELF:
            greet(half, z, along(k))
        greet(1 - half, z, along(k))
    for dz in range(1, SIDE):
        greet(half, lax.rem(z + dz, SIDE), y)
    rates[1].start()
    for copy in others:
        copy.start()
    for c in range(CHUNKS):
        load(k_hbm, kb, k_sem, 1, c).start()
        load(v_hbm, vb, v_sem, 1, c).start()
    for p in range(2):
        for c in range(CHUNKS):
            load(q_hbm, qb, q_sem, p, c).start()

    def turn(src, dst, place):
        for b in range(SUBS):
            lanes = pl.ds(b * LANES, LANES)
            for m in range(0, MODES, SUBS):
                at = pl.ds((place * MODES + m) * SUBS + b, SUBS, stride=SUBS)
                dst[at, :] = src[place, m : m + SUBS, lanes]

    modes = [along(k) * OWNED + e for k in range(SIDE) for e in range(OWNED)]

    def decays(place):
        for n, m in enumerate(modes):
            fade[reg(place, n), :] = jnp.exp(-rate[reg(place, m), :])

    rates[0].wait()
    turn(db, rate, 0)
    decays(0)
    for n, m in enumerate(modes):
        fade8[reg(0, n), :] = jnp.exp(-float(BLOCK) * rate[reg(0, m), :])

    def arrive(place, c):
        load(k_hbm, kb, k_sem, place, c).wait()
        load(v_hbm, vb, v_sem, place, c).wait()

    def spread(place, t, to):
        for b in range(SUBS):
            lanes = pl.ds(b * LANES, LANES)
            for i in range(0, STEP, TILE):
                at = pl.ds(t + i, TILE)
                x = kb[place, at, lanes].astype(F32) * vb[place, at, lanes].astype(F32)
                for j in range(0, TILE, SUBS):
                    xb[tile(place, to + i + j, b), :] = x[j : j + SUBS]

    def read(place, t):
        return [xb[row(place, t + j), :] for j in range(BLOCK)]

    def gather(slots, look, first, size, held):
        step = STEP if look else WIDE

        def body(i, held):
            t = pl.multiple_of(first + i * step, step)
            held = list(held)
            for s in range(0, step, BLOCK):
                xs = read(0, t + s)
                for at, n in enumerate(slots):
                    a = fade[reg(0, n), :]
                    e = xs[0]
                    for x in xs[1:]:
                        e = e * a + x
                    left[(t + s) // BLOCK, n] = e
                    held[at] = held[at] * fade8[reg(0, n), :] + e
            if look:
                spread(0, pl.multiple_of(jnp.minimum(t + STEP, first + size - STEP), STEP), t + STEP)
            return tuple(held)

        return lax.fori_loop(0, size // step, body, held)

    zeros = jnp.zeros((SUBS, LANES), F32)

    def leave(slots, held):
        for at, n in enumerate(slots):
            ends[n] = held[at]

    slots = range(2 * OWNED)
    held = (zeros,) * len(slots)
    for c in range(CHUNKS):
        arrive(0, c)
        spread(0, c * chunk, c * chunk)
        held = gather(slots, True, c * chunk, chunk, held)
    leave(slots, held)
    far = (y > 0) & (z > 0)

    @pl.when(far)
    def _():
        pl.semaphore_wait(barrier, 3 * SIDE - 2)
        to_owner(0).start()
        to_owner(1).start()

    for k in range(2, SIDE):
        slots = range(k * OWNED, (k + 1) * OWNED)
        leave(slots, gather(slots, False, 0, ROWS, (zeros,) * OWNED))
        if k != SELF:

            @pl.when(far)
            def _(k=k):
                to_owner(k).start()

            @pl.when(~far)
            def _():
                pl.semaphore_wait(barrier, 3 * SIDE - 2)
                to_owner(0).start()
                to_owner(1).start()
                to_owner(2).start()

    for e in range(OWNED):
        heard[y, e] = ends[SELF * OWNED + e]

    rates[1].wait()
    turn(db, rate, 1)
    decays(1)
    for copy in others:
        copy.wait()
    for place in range(2):
        turn(rb, raw, place)
        for n, m in enumerate(modes):
            amp[reg(place, n), :] = raw[reg(place, m), :] * jnp.sqrt(rate[reg(place, m), :])
    terms = [amp[reg(0, n), :] for n in range(MODES)]
    for j in range(BLOCK):
        total = sum(terms[1:], terms[0])
        taps[reg(0, j), :] = total + gb[0] if j == 0 else total
        if j < BLOCK - 1:
            terms = [term * fade[reg(0, n), :] for n, term in enumerate(terms)]
        if j == 0:
            for n, term in enumerate(terms):
                lead[reg(0, n), :] = term

    def own(i, carry):
        t = pl.multiple_of(i * STEP, STEP)
        for s in range(0, STEP, BLOCK):
            xs = read(0, t + s)
            for j in range(BLOCK):
                out = taps[reg(0, 0), :] * xs[j]
                for i in range(j):
                    out = out + taps[reg(0, j - i), :] * xs[i]
                xb[row(0, t + s + j), :] = out
        return carry

    def other(i, held):
        t = pl.multiple_of(i * STEP, STEP)
        held = list(held)
        g = gb[1]
        for s in range(0, STEP, BLOCK):
            xs = read(1, t + s)
            ys = [g * x for x in xs]
            for n in range(MODES):
                a = fade[reg(1, n), :]
                w = amp[reg(1, n), :]
                for j in range(BLOCK):
                    held[n] = held[n] * a + xs[j]
                    ys[j] = ys[j] + w * held[n]
            for j in range(BLOCK):
                xb[row(1, t + s + j), :] = ys[j]
        spread(1, pl.multiple_of(jnp.minimum(t + STEP, ROWS - STEP), STEP), t + STEP)
        return tuple(held)

    steps = ROWS // STEP

    def by_place(*choices):
        return jnp.where(y < 2, jnp.where(y == 0, choices[0], choices[1]), jnp.where(y == 2, choices[2], choices[3]))

    part_a = by_place(7, 4, 4, 2)
    part_b = jnp.where(z == 0, part_a, jnp.where(z == SIDE - 1, by_place(13, 10, 9, 8), by_place(11, 8, 9, 7)))

    lax.fori_loop(0, steps, own, 0)
    for c in range(CHUNKS):
        arrive(1, c)
    spread(1, 0, 0)
    held = lax.fori_loop(0, part_a, other, (zeros,) * MODES)

    for k in range(SIDE):
        if k != SELF:
            to_owner(k).wait()
    for e in range(OWNED):
        whole = jnp.exp(-float(ROWS) * rate[reg(0, y * OWNED + e), :])
        total = zeros
        for place in range(SIDE):
            before[place, e] = total
            total = total * whole + heard[place, e]
        sums[e] = total
    for dz in range(1, SIDE):

        @pl.when(z + dz < SIDE)
        def _(dz=dz):
            to_later(dz).start()

    held = lax.fori_loop(part_a, part_b, other, held)

    for dz in range(1, SIDE):

        @pl.when(z - dz >= 0)
        def _(dz=dz):
            to_later(dz).wait_recv()

    for e in range(OWNED):
        d = rate[reg(0, y * OWNED + e), :]
        row_long = jnp.exp(-float(SIDE * ROWS) * d)
        whole = jnp.exp(-float(ROWS) * d)
        total = lax.fori_loop(0, z, lambda i, total: total * row_long + earlier[i, e], zeros)
        for place in range(SIDE):
            starts[place, e] = total + before[place, e]
            total = total * whole
    for k in range(SIDE):
        if k != SELF:
            to_same(k).start()
        to_twin(k).start()
    for e in range(OWNED):
        enter[0, SELF * OWNED + e] = starts[y, e]

    lax.fori_loop(part_b, steps, other, held)

    for dz in range(1, SIDE):

        @pl.when(z + dz < SIDE)
        def _(dz=dz):
            to_later(dz).wait_send()

    def pour(blocks):
        slots = [k * OWNED + e for k in blocks for e in range(OWNED)]

        def body(i, state):
            t = pl.multiple_of(i * WIDE, WIDE)
            state = list(state)
            for s in range(0, WIDE, BLOCK):
                ys = read(0, t + s)
                for at, n in enumerate(slots):
                    a = fade[reg(0, n), :]
                    now = state[at] * lead[reg(0, n), :]
                    ys[0] = ys[0] + now
                    for j in range(1, BLOCK):
                        now = now * a
                        ys[j] = ys[j] + now
                    state[at] = state[at] * fade8[reg(0, n), :] + left[(t + s) // BLOCK, n]
                for j in range(BLOCK):
                    xb[row(0, t + s + j), :] = ys[j]
            return tuple(state)

        lax.fori_loop(0, ROWS // WIDE, body, tuple(enter[0, n] for n in slots))

    pour((SELF,))
    for p in range(2):
        for c in range(CHUNKS):
            load(q_hbm, qb, q_sem, p, c).wait()
    for k in range(SIDE):
        if k != SELF:
            to_same(k).wait_send()
        to_twin(k).wait_send()
    for k in (2, 1, 0):
        to_same(BACK[k]).wait_recv()
        pour((k,))
    for k in range(SIDE):
        to_twin(k).wait_recv()


def second_kernel(xs, enter, fade, amp, qb, o_hbm, xb, state, ob, o_sem):
    group = SUBS * LANES
    chunk = ROWS // PARTS
    half = lax.axis_index("half")
    owner = (half, 1 - half)

    def store(place, c):
        at = pl.ds(c * chunk, chunk)
        columns = pl.ds(pl.multiple_of(owner[place] * group, group), group)
        return pltpu.make_async_copy(ob.at[place, at, :], o_hbm.at[at, columns], o_sem.at[place, c])

    def gate(place, t, turned):
        for b in range(SUBS):
            lanes = pl.ds(b * LANES, LANES)
            out = jnp.concatenate([turned(j, b) for j in range(0, TILE, SUBS)])
            ob[place, pl.ds(t, TILE), lanes] = (qb[place, pl.ds(t, TILE), lanes].astype(F32) * out).astype(jnp.bfloat16)

    for n in range(MODES):
        state[n] = amp[reg(1, n), :] * enter[1, n]
    for c in range(PARTS):

        def body(i, carry, first=c * chunk):
            t = pl.multiple_of(first + i * STEP, STEP)
            for s in range(0, STEP, BLOCK):
                ys = [xs[row(1, t + s + j), :] for j in range(BLOCK)]
                for n in range(MODES):
                    a = fade[reg(1, n), :]
                    now = state[n]
                    for j in range(BLOCK):
                        now = now * a
                        ys[j] = ys[j] + now
                    state[n] = now
                for j in range(BLOCK):
                    xb[pl.ds((s + j) * SUBS, SUBS), :] = ys[j]
                if (s + BLOCK) % TILE == 0:
                    at = s + BLOCK - TILE
                    gate(0, t + at, lambda j, b, at=at: xs[tile(0, t + at + j, b), :])
                    gate(1, t + at, lambda j, b, at=at: xb[pl.ds((at + j) * SUBS + b, SUBS, stride=SUBS), :])
            return carry

        lax.fori_loop(0, chunk // STEP, body, 0)
        store(0, c).start()
        store(1, c).start()
    for place in range(2):
        for c in range(PARTS):
            store(place, c).wait()


def shards(query_gate, key_gate, value_input, residues, decays, skip_gain):
    rows, width = key_gate.shape
    group = width // 2
    assert group == SUBS * LANES and rows == ROWS
    assert residues.shape[0] == MODES and lax.axis_size("ctx") == SIDE * SIDE
    wide = pltpu.VMEM((2, rows, group), jnp.bfloat16)
    table = (2 * MODES * SUBS, LANES)
    dma = pltpu.SemaphoreType.DMA
    hbm = pl.BlockSpec(memory_space=pltpu.HBM)
    vmem = pl.BlockSpec(memory_space=pltpu.VMEM)

    def registers(*shape):
        return pltpu.VMEM((*shape, SUBS, LANES), F32)

    operands = (query_gate, key_gate, value_input, residues, decays, skip_gain.reshape(2 * SUBS, LANES))
    kept = pl.pallas_call(
        first_kernel,
        out_shape=[
            jax.ShapeDtypeStruct((2 * SPAN * SUBS, LANES), F32),
            jax.ShapeDtypeStruct((2, MODES, SUBS, LANES), F32),
            jax.ShapeDtypeStruct(table, F32),
            jax.ShapeDtypeStruct(table, F32),
            jax.ShapeDtypeStruct((2, rows, group), jnp.bfloat16),
        ],
        in_specs=[hbm] * 6,
        out_specs=[vmem] * 5,
        scratch_shapes=[wide, wide]
        + [pltpu.VMEM((2, MODES, group), F32)] * 2
        + [registers(2)]
        + [pltpu.VMEM(table, F32)] * 5
        + [
            registers(rows // BLOCK, MODES),
            registers(MODES),
            registers(SIDE, OWNED),
            registers(OWNED),
            registers(SIDE, OWNED),
            registers(SIDE, OWNED),
            registers(SIDE, OWNED),
            dma((2, 3)),
        ]
        + [dma((2, CHUNKS))] * 3
        + [dma((SIDE,))] * 8,
        compiler_params=pltpu.CompilerParams(
            collective_id=0, has_side_effects=True, vmem_limit_bytes=FIRST_VMEM
        ),
    )(*(pltpu.with_memory_space_constraint(x, pltpu.HBM) for x in operands))
    return pl.pallas_call(
        second_kernel,
        out_shape=jax.ShapeDtypeStruct((rows, width), jnp.bfloat16),
        in_specs=[vmem] * 5,
        out_specs=hbm,
        scratch_shapes=[pltpu.VMEM((STEP * SUBS, LANES), F32), registers(MODES), wide, dma((2, PARTS))],
        compiler_params=pltpu.CompilerParams(vmem_limit_bytes=SECOND_VMEM),
    )(*kept)


def solution(mesh):
    placed = (
        P("ctx", "chan"),
        P("ctx", "chan"),
        P("ctx", "chan"),
        P(None, "chan"),
        P(None, "chan"),
        P("chan"),
    )
    return jax.shard_map(shards, mesh=mesh, in_specs=placed, out_specs=P("ctx", "chan"), check_vma=False)
```

```python
import jax
import jax.numpy as jnp
from jax import lax
from jax.experimental import pallas as pl
from jax.experimental.pallas import tpu as pltpu
from jax.sharding import PartitionSpec as P

F32 = jnp.float32
LANES = 128
SUBS = 8
TILE = 16
BLOCK = 8
STEP = 32
WIDE = 64
ROWS = 512
SPAN = ROWS + STEP
CHUNKS = 4
PARTS = 8
SIDE = 4
MODES = 16
OWNED = MODES // SIDE
AWAY = (2, 1, 3, 0)
BACK = tuple(AWAY.index(-a % SIDE) for a in AWAY)
SELF = SIDE - 1
FIRST_VMEM = 36 << 20
SECOND_VMEM = 36 << 20


def reg(place, n):
    return pl.ds(pl.multiple_of((place * MODES + n) * SUBS, SUBS), SUBS)


def row(place, t):
    return pl.ds(pl.multiple_of((place * SPAN + t) * SUBS, SUBS), SUBS)


def tile(place, t, b):
    return pl.ds((place * SPAN + t) * SUBS + b, SUBS, stride=SUBS)


def first_kernel(
    q_hbm, k_hbm, v_hbm, r_hbm, d_hbm, g_hbm, xb, enter, fade, amp, qb,
    kb, vb, rb, db, gb, rate, raw, fade8, lead, taps, left, ends, heard, sums, earlier, before, starts,
    p_sem, k_sem, v_sem, q_sem, a_send, a_recv, b_send, b_recv, c_send, c_recv, t_send, t_recv,
):
    group = SUBS * LANES
    chunk = ROWS // CHUNKS
    half = lax.axis_index("half")
    ctx = lax.axis_index("ctx")
    z = ctx // SIDE
    y = lax.rem(ctx, SIDE)
    owner = (half, 1 - half)

    def columns(place):
        return pl.ds(pl.multiple_of(owner[place] * group, group), group)

    def load(hbm, buf, sem, place, c):
        at = pl.ds(c * chunk, chunk)
        return pltpu.make_async_copy(hbm.at[at, columns(place)], buf.at[place, at, :], sem.at[place, c])

    def remote(src, dst, send_sem, recv_sem, to_half, to_z, to_y):
        return pltpu.make_async_remote_copy(
            src_ref=src,
            dst_ref=dst,
            send_sem=send_sem,
            recv_sem=recv_sem,
            device_id={"half": to_half, "ctx": to_z * SIDE + to_y},
            device_id_type=pl.DeviceIdType.MESH,
        )

    def along(k):
        return lax.rem(y + AWAY[k], SIDE)

    def to_owner(k):
        return remote(
            ends.at[pl.ds(k * OWNED, OWNED)], heard.at[y], a_send.at[k], a_recv.at[k], half, z, along(k)
        )

    def to_later(dz):
        return remote(sums, earlier.at[z], b_send.at[dz - 1], b_recv.at[dz - 1], half, lax.rem(z + dz, SIDE), y)

    def to_same(k):
        return remote(
            starts.at[along(k)], enter.at[0, pl.ds(BACK[k] * OWNED, OWNED)], c_send.at[k], c_recv.at[k], half, z, along(k)
        )

    def to_twin(k):
        return remote(
            starts.at[along(k)], enter.at[1, pl.ds(BACK[k] * OWNED, OWNED)], t_send.at[k], t_recv.at[k], 1 - half, z, along(k)
        )

    barrier = pltpu.get_barrier_semaphore()

    def greet(to_half, to_z, to_y):
        pl.semaphore_signal(
            barrier,
            inc=1,
            device_id={"half": to_half, "ctx": to_z * SIDE + to_y},
            device_id_type=pl.DeviceIdType.MESH,
        )

    rates = [pltpu.make_async_copy(d_hbm.at[:, columns(p)], db.at[p], p_sem.at[p, 0]) for p in range(2)]
    others = [pltpu.make_async_copy(r_hbm.at[:, columns(p)], rb.at[p], p_sem.at[p, 1]) for p in range(2)]
    others += [
        pltpu.make_async_copy(
            g_hbm.at[pl.ds(pl.multiple_of(owner[p] * SUBS, SUBS), SUBS), :], gb.at[p], p_sem.at[p, 2]
        )
        for p in range(2)
    ]
    rates[0].start()
    for c in range(CHUNKS):
        load(k_hbm, kb, k_sem, 0, c).start()
        load(v_hbm, vb, v_sem, 0, c).start()
    for k in range(SIDE):
        if k != SELF:
            greet(half, z, along(k))
        greet(1 - half, z, along(k))
    for dz in range(1, SIDE):
        greet(half, lax.rem(z + dz, SIDE), y)
    rates[1].start()
    for copy in others:
        copy.start()
    for c in range(CHUNKS):
        load(k_hbm, kb, k_sem, 1, c).start()
        load(v_hbm, vb, v_sem, 1, c).start()
    for p in range(2):
        for c in range(CHUNKS):
            load(q_hbm, qb, q_sem, p, c).start()

    def turn(src, dst, place):
        for b in range(SUBS):
            lanes = pl.ds(b * LANES, LANES)
            for m in range(0, MODES, SUBS):
                at = pl.ds((place * MODES + m) * SUBS + b, SUBS, stride=SUBS)
                dst[at, :] = src[place, m : m + SUBS, lanes]

    modes = [along(k) * OWNED + e for k in range(SIDE) for e in range(OWNED)]

    def decays(place):
        for n, m in enumerate(modes):
            fade[reg(place, n), :] = jnp.exp(-rate[reg(place, m), :])

    rates[0].wait()
    turn(db, rate, 0)
    decays(0)
    for n, m in enumerate(modes):
        fade8[reg(0, n), :] = jnp.exp(-float(BLOCK) * rate[reg(0, m), :])

    def arrive(place, c):
        load(k_hbm, kb, k_sem, place, c).wait()
        load(v_hbm, vb, v_sem, place, c).wait()

    def spread(place, t, to):
        for b in range(SUBS):
            lanes = pl.ds(b * LANES, LANES)
            for i in range(0, STEP, TILE):
                at = pl.ds(t + i, TILE)
                x = kb[place, at, lanes].astype(F32) * vb[place, at, lanes].astype(F32)
                for j in range(0, TILE, SUBS):
                    xb[tile(place, to + i + j, b), :] = x[j : j + SUBS]

    def read(place, t):
        return [xb[row(place, t + j), :] for j in range(BLOCK)]

    def gather(slots, look, first, size, held):
        step = STEP if look else WIDE

        def body(i, held):
            t = pl.multiple_of(first + i * step, step)
            held = list(held)
            for s in range(0, step, BLOCK):
                xs = read(0, t + s)
                for at, n in enumerate(slots):
                    a = fade[reg(0, n), :]
                    e = xs[0]
                    for x in xs[1:]:
                        e = e * a + x
                    left[(t + s) // BLOCK, n] = e
                    held[at] = held[at] * fade8[reg(0, n), :] + e
            if look:
                spread(0, pl.multiple_of(jnp.minimum(t + STEP, first + size - STEP), STEP), t + STEP)
            return tuple(held)

        return lax.fori_loop(0, size // step, body, held)

    zeros = jnp.zeros((SUBS, LANES), F32)

    def leave(slots, held):
        for at, n in enumerate(slots):
            ends[n] = held[at]

    slots = range(2 * OWNED)
    held = (zeros,) * len(slots)
    for c in range(CHUNKS):
        arrive(0, c)
        spread(0, c * chunk, c * chunk)
        held = gather(slots, True, c * chunk, chunk, held)
    leave(slots, held)
    far = (y > 0) & (z > 0)

    @pl.when(far)
    def _():
        pl.semaphore_wait(barrier, 3 * SIDE - 2)
        to_owner(0).start()
        to_owner(1).start()

    for k in range(2, SIDE):
        slots = range(k * OWNED, (k + 1) * OWNED)
        leave(slots, gather(slots, False, 0, ROWS, (zeros,) * OWNED))
        if k != SELF:

            @pl.when(far)
            def _(k=k):
                to_owner(k).start()

            @pl.when(~far)
            def _():
                pl.semaphore_wait(barrier, 3 * SIDE - 2)
                to_owner(0).start()
                to_owner(1).start()
                to_owner(2).start()

    for e in range(OWNED):
        heard[y, e] = ends[SELF * OWNED + e]

    rates[1].wait()
    turn(db, rate, 1)
    decays(1)
    for copy in others:
        copy.wait()
    for place in range(2):
        turn(rb, raw, place)
        for n, m in enumerate(modes):
            amp[reg(place, n), :] = raw[reg(place, m), :] * jnp.sqrt(rate[reg(place, m), :])
    terms = [amp[reg(0, n), :] for n in range(MODES)]
    for j in range(BLOCK):
        total = sum(terms[1:], terms[0])
        taps[reg(0, j), :] = total + gb[0] if j == 0 else total
        if j < BLOCK - 1:
            terms = [term * fade[reg(0, n), :] for n, term in enumerate(terms)]
        if j == 0:
            for n, term in enumerate(terms):
                lead[reg(0, n), :] = term

    def own(i, carry):
        t = pl.multiple_of(i * STEP, STEP)
        for s in range(0, STEP, BLOCK):
            xs = read(0, t + s)
            for j in range(BLOCK):
                out = taps[reg(0, 0), :] * xs[j]
                for i in range(j):
                    out = out + taps[reg(0, j - i), :] * xs[i]
                xb[row(0, t + s + j), :] = out
        return carry

    def other(i, held):
        t = pl.multiple_of(i * STEP, STEP)
        held = list(held)
        g = gb[1]
        for s in range(0, STEP, BLOCK):
            xs = read(1, t + s)
            ys = [g * x for x in xs]
            for n in range(MODES):
                a = fade[reg(1, n), :]
                w = amp[reg(1, n), :]
                for j in range(BLOCK):
                    held[n] = held[n] * a + xs[j]
                    ys[j] = ys[j] + w * held[n]
            for j in range(BLOCK):
                xb[row(1, t + s + j), :] = ys[j]
        spread(1, pl.multiple_of(jnp.minimum(t + STEP, ROWS - STEP), STEP), t + STEP)
        return tuple(held)

    steps = ROWS // STEP

    def by_place(*choices):
        return jnp.where(y < 2, jnp.where(y == 0, choices[0], choices[1]), jnp.where(y == 2, choices[2], choices[3]))

    part_a = by_place(7, 4, 4, 2)
    part_b = jnp.where(z == 0, part_a, jnp.where(z == SIDE - 1, by_place(13, 10, 9, 8), by_place(11, 8, 9, 7)))

    lax.fori_loop(0, steps, own, 0)
    for c in range(CHUNKS):
        arrive(1, c)
    spread(1, 0, 0)
    held = lax.fori_loop(0, part_a, other, (zeros,) * MODES)

    for k in range(SIDE):
        if k != SELF:
            to_owner(k).wait()
    for e in range(OWNED):
        whole = jnp.exp(-float(ROWS) * rate[reg(0, y * OWNED + e), :])
        total = zeros
        for place in range(SIDE):
            before[place, e] = total
            total = total * whole + heard[place, e]
        sums[e] = total
    for dz in range(1, SIDE):

        @pl.when(z + dz < SIDE)
        def _(dz=dz):
            to_later(dz).start()

    held = lax.fori_loop(part_a, part_b, other, held)

    for dz in range(1, SIDE):

        @pl.when(z - dz >= 0)
        def _(dz=dz):
            to_later(dz).wait_recv()

    for e in range(OWNED):
        d = rate[reg(0, y * OWNED + e), :]
        row_long = jnp.exp(-float(SIDE * ROWS) * d)
        whole = jnp.exp(-float(ROWS) * d)
        total = lax.fori_loop(0, z, lambda i, total: total * row_long + earlier[i, e], zeros)
        for place in range(SIDE):
            starts[place, e] = total + before[place, e]
            total = total * whole
    for k in range(SIDE):
        if k != SELF:
            to_same(k).start()
        to_twin(k).start()
    for e in range(OWNED):
        enter[0, SELF * OWNED + e] = starts[y, e]

    lax.fori_loop(part_b, steps, other, held)

    for dz in range(1, SIDE):

        @pl.when(z + dz < SIDE)
        def _(dz=dz):
            to_later(dz).wait_send()

    def pour(blocks):
        slots = [k * OWNED + e for k in blocks for e in range(OWNED)]

        def body(i, state):
            t = pl.multiple_of(i * WIDE, WIDE)
            state = list(state)
            for s in range(0, WIDE, BLOCK):
                ys = read(0, t + s)
                for at, n in enumerate(slots):
                    a = fade[reg(0, n), :]
                    now = state[at] * lead[reg(0, n), :]
                    ys[0] = ys[0] + now
                    for j in range(1, BLOCK):
                        now = now * a
                        ys[j] = ys[j] + now
                    state[at] = state[at] * fade8[reg(0, n), :] + left[(t + s) // BLOCK, n]
                for j in range(BLOCK):
                    xb[row(0, t + s + j), :] = ys[j]
            return tuple(state)

        lax.fori_loop(0, ROWS // WIDE, body, tuple(enter[0, n] for n in slots))

    pour((SELF,))
    for p in range(2):
        for c in range(CHUNKS):
            load(q_hbm, qb, q_sem, p, c).wait()
    for k in range(SIDE):
        if k != SELF:
            to_same(k).wait_send()
        to_twin(k).wait_send()
    for k in (2, 1, 0):
        to_same(BACK[k]).wait_recv()
        pour((k,))
    for k in range(SIDE):
        to_twin(k).wait_recv()


def second_kernel(xs, enter, fade, amp, qb, o_hbm, xb, state, ob, o_sem):
    group = SUBS * LANES
    chunk = ROWS // PARTS
    half = lax.axis_index("half")
    owner = (half, 1 - half)

    def store(place, c):
        at = pl.ds(c * chunk, chunk)
        columns = pl.ds(pl.multiple_of(owner[place] * group, group), group)
        return pltpu.make_async_copy(ob.at[place, at, :], o_hbm.at[at, columns], o_sem.at[place, c])

    def gate(place, t, turned):
        for b in range(SUBS):
            lanes = pl.ds(b * LANES, LANES)
            out = jnp.concatenate([turned(j, b) for j in range(0, TILE, SUBS)])
            ob[place, pl.ds(t, TILE), lanes] = (qb[place, pl.ds(t, TILE), lanes].astype(F32) * out).astype(jnp.bfloat16)

    for n in range(MODES):
        state[n] = amp[reg(1, n), :] * enter[1, n]
    for c in range(PARTS):

        def body(i, carry, first=c * chunk):
            t = pl.multiple_of(first + i * WIDE, WIDE)
            for s in range(0, WIDE, BLOCK):
                ys = [xs[row(1, t + s + j), :] for j in range(BLOCK)]
                for n in range(MODES):
                    a = fade[reg(1, n), :]
                    now = state[n]
                    for j in range(BLOCK):
                        now = now * a
                        ys[j] = ys[j] + now
                    state[n] = now
                for j in range(BLOCK):
                    xb[pl.ds((s + j) * SUBS, SUBS), :] = ys[j]
                if (s + BLOCK) % TILE == 0:
                    at = s + BLOCK - TILE
                    gate(0, t + at, lambda j, b, at=at: xs[tile(0, t + at + j, b), :])
                    gate(1, t + at, lambda j, b, at=at: xb[pl.ds((at + j) * SUBS + b, SUBS, stride=SUBS), :])
            return carry

        lax.fori_loop(0, chunk // WIDE, body, 0)
        store(0, c).start()
        store(1, c).start()
    for place in range(2):
        for c in range(PARTS):
            store(place, c).wait()


def shards(query_gate, key_gate, value_input, residues, decays, skip_gain):
    rows, width = key_gate.shape
    group = width // 2
    assert group == SUBS * LANES and rows == ROWS
    assert residues.shape[0] == MODES and lax.axis_size("ctx") == SIDE * SIDE
    wide = pltpu.VMEM((2, rows, group), jnp.bfloat16)
    table = (2 * MODES * SUBS, LANES)
    dma = pltpu.SemaphoreType.DMA
    hbm = pl.BlockSpec(memory_space=pltpu.HBM)
    vmem = pl.BlockSpec(memory_space=pltpu.VMEM)

    def registers(*shape):
        return pltpu.VMEM((*shape, SUBS, LANES), F32)

    operands = (query_gate, key_gate, value_input, residues, decays, skip_gain.reshape(2 * SUBS, LANES))
    kept = pl.pallas_call(
        first_kernel,
        out_shape=[
            jax.ShapeDtypeStruct((2 * SPAN * SUBS, LANES), F32),
            jax.ShapeDtypeStruct((2, MODES, SUBS, LANES), F32),
            jax.ShapeDtypeStruct(table, F32),
            jax.ShapeDtypeStruct(table, F32),
            jax.ShapeDtypeStruct((2, rows, group), jnp.bfloat16),
        ],
        in_specs=[hbm] * 6,
        out_specs=[vmem] * 5,
        scratch_shapes=[wide, wide]
        + [pltpu.VMEM((2, MODES, group), F32)] * 2
        + [registers(2)]
        + [pltpu.VMEM(table, F32)] * 5
        + [
            registers(rows // BLOCK, MODES),
            registers(MODES),
            registers(SIDE, OWNED),
            registers(OWNED),
            registers(SIDE, OWNED),
            registers(SIDE, OWNED),
            registers(SIDE, OWNED),
            dma((2, 3)),
        ]
        + [dma((2, CHUNKS))] * 3
        + [dma((SIDE,))] * 8,
        compiler_params=pltpu.CompilerParams(
            collective_id=0, has_side_effects=True, vmem_limit_bytes=FIRST_VMEM
        ),
    )(*(pltpu.with_memory_space_constraint(x, pltpu.HBM) for x in operands))
    return pl.pallas_call(
        second_kernel,
        out_shape=jax.ShapeDtypeStruct((rows, width), jnp.bfloat16),
        in_specs=[vmem] * 5,
        out_specs=hbm,
        scratch_shapes=[pltpu.VMEM((WIDE * SUBS, LANES), F32), registers(MODES), wide, dma((2, PARTS))],
        compiler_params=pltpu.CompilerParams(vmem_limit_bytes=SECOND_VMEM),
    )(*kept)


def solution(mesh):
    placed = (
        P("ctx", "chan"),
        P("ctx", "chan"),
        P("ctx", "chan"),
        P(None, "chan"),
        P(None, "chan"),
        P("chan"),
    )
    return jax.shard_map(shards, mesh=mesh, in_specs=placed, out_specs=P("ctx", "chan"), check_vma=False)
```
